128 devices in a mesh: lat: 32 (over z, x, core), lev: 4 (over y).
Axes of the slice: x: 4, y: 4, z: 4, core: 2. Of those that a mesh axis runs over, the one named last changes fastest.
Arguments:
- fields: float32 [3, 16, 1024, 4096], P(None, 'lev', 'lat'), may hold values from -6 to 6
- velocity: float32 [2, 16, 1024, 4096], P(None, 'lev', 'lat'), may hold values from -6 to 6
- surface: float32 [1024, 4096], P('lat'), may hold values from -6 to 6
- thickness: float32 [16], P('lev'), may hold values from 0.02 to 0.2
- row_owner: int32 [1024], P('lat'), may hold values from -1 to 31, as said below
Outputs:
- new_fields: float32 [3, 16, 1024, 4096], P(None, 'lev', 'lat')
- geopotential: float32 [16, 1024, 4096], P('lev', 'lat')
- polar_rows: float32 [3, 16, 512, 4096], P(None, 'lev', 'lat')
The draws below stay inside these ranges and needn't reach their ends.
Inputs may be any that keep to these rules, and one draw needn't show every extreme that they name: `row_owner`: exactly the rows j < 256 and j >= 768 hold a device index, all others -1. Of the rows held by one device p, exactly 16 name p and the other 16 name the device (p + 32 / 2) mod 32.
All inputs are finite; a program needn't handle non-finite values.
Results may differ from the reference program's by a relative error of at most 0.0003.
Values sent between devices are 32-bit elements; how exact they have to be, the bound alone decides.
A program may use at most 128 MiB of HBM per device.

```python
import math
import jax
import jax.numpy as jnp

NF = 3
NLON = 4096
LAT_DEV = 32
PASSES = 8
NLAT = 1024
LEVELS = 16


def draw_row_owner(key, part):
    groups = NLAT // LAT_DEV
    quarter = groups // 4
    half_rows = LAT_DEV // 2
    polar_ids = jnp.concatenate([jnp.arange(quarter), jnp.arange(groups - quarter, groups)]).astype(jnp.int32)

    def one_device(device):
        local_key = jax.random.fold_in(jax.random.fold_in(key, 17), device)
        shuffled = jax.random.permutation(local_key, LAT_DEV)
        partner = (device + groups // 2) % groups
        targets = jnp.concatenate([jnp.full((half_rows,), device, jnp.int32), jnp.full((half_rows,), partner, jnp.int32)])
        return jnp.zeros((LAT_DEV,), jnp.int32).at[shuffled].set(targets)
    blocks = jax.vmap(one_device)(polar_ids)
    table = jnp.full((groups, LAT_DEV), -1, jnp.int32)
    table = table.at[polar_ids].set(blocks)
    return table.reshape(NLAT)


def steps_of(rng, shape, split, low, largest):
    def one(axis_at, shards_of):
        steps = jax.random.uniform(jax.random.fold_in(jax.random.fold_in(rng, 6), axis_at), (shards_of,), jnp.float32, low / len(split), largest / len(split))
        return jnp.repeat(jnp.exp(steps), shape[axis_at] // shards_of).reshape((-1,) + (1,) * (len(shape) - axis_at - 1))

    gain = one(*split[0])
    for cut in split[1:]:
        gain = gain * one(*cut)
    return gain


def bell_draw(key, extent, spread, limit, pieces=(), kind=jnp.bfloat16):
    drawn = spread * jax.random.normal(key, extent, jnp.float32)
    if pieces:
        drawn = drawn * steps_of(key, extent, pieces, -0.22, 0.18)
    return jnp.clip(drawn, -limit, limit).astype(kind)


def setup_inputs(seed: int = 0) -> dict:
    key_list = jax.random.split(jax.random.key(seed), 6)
    fields = bell_draw(key_list[0], (NF, LEVELS, NLAT, NLON), 1.0, 6.0, ((1, 4), (2, 32)), jnp.float32)
    velocity = bell_draw(key_list[1], (2, LEVELS, NLAT, NLON), 1.0, 6.0, ((1, 4), (2, 32)), jnp.float32)
    surface = bell_draw(key_list[2], (NLAT, NLON), 1.0, 6.0, ((0, 32),), jnp.float32)
    thickness = jnp.clip(jnp.exp(math.log(0.2) - 2.3025851 * jax.random.uniform(key_list[3], (LEVELS,), jnp.float32) ** steps_of(key_list[3], (LEVELS,), ((0, 4),), -0.2, 0.2)), 0.02, 0.2)
    row_owner = draw_row_owner(jax.random.fold_in(key_list[5], 71), 0)
    return dict(fields=fields, velocity=velocity, surface=surface, thickness=thickness, row_owner=row_owner)


courant_lon = 0.3
courant_lat = 0.3
diffuse_lon = 0.04
diffuse_lat = 0.08
base_temp = 3.0


def row_tables(start, row_count, all_rows):
    row_index = start + jnp.arange(row_count)
    row_ids = row_index.astype(jnp.float32)
    spacing = math.pi / all_rows
    lat_mid = -0.5 * math.pi + (row_ids + 0.5) * spacing
    cos_mid = jnp.cos(lat_mid)
    metric = 1.0 / jnp.maximum(cos_mid, 0.25)
    cos_north = jnp.cos(lat_mid + 0.5 * spacing)
    cos_south = jnp.cos(lat_mid - 0.5 * spacing)
    polar = (row_index < all_rows // 4) | (row_index >= all_rows - all_rows // 4)
    strength = jnp.where(polar, 0.05 + 0.2 * (1.0 - cos_mid / math.cos(0.25 * math.pi)), 0.0)
    return metric[:, None], cos_north[:, None], cos_south[:, None], strength[:, None]


def advect(state, wind_u, wind_v, north_rows, south_rows, metric, cos_north, cos_south):
    east_cell = jnp.roll(state, -1, axis=-1)
    west_cell = jnp.roll(state, 1, axis=-1)
    result = state - courant_lon * metric * wind_u * (east_cell - west_cell) * 0.5
    result = result - courant_lat * wind_v * (north_rows - south_rows) * 0.5
    result = result + diffuse_lon * metric * metric * (east_cell - 2.0 * state + west_cell)
    return result + diffuse_lat * metric * (cos_north * (north_rows - state) - cos_south * (state - south_rows))


def minmod(left_val, right_val):
    return 0.5 * (jnp.sign(left_val) + jnp.sign(right_val)) * jnp.minimum(jnp.abs(left_val), jnp.abs(right_val))


def smooth(state, strength):
    for pass_index in range(PASSES):
        slopes = jnp.roll(state, -1, axis=-1) - state
        limited = minmod(slopes, minmod(jnp.roll(slopes, 1, axis=-1), jnp.roll(slopes, -1, axis=-1)))
        fluxes = strength * (slopes - limited)
        state = state + fluxes - jnp.roll(fluxes, 1, axis=-1)
    return state


def reference(fields, velocity, surface, thickness, row_owner):
    all_rows = fields.shape[2]
    metric, cos_north, cos_south, strength = row_tables(0, all_rows, all_rows)
    new_levels = []
    weights = []
    for level in range(LEVELS):
        state = fields[:, level]
        north_rows = jnp.concatenate([state[:, 1:], state[:, -1:]], axis=1)
        south_rows = jnp.concatenate([state[:, :1], state[:, :-1]], axis=1)
        moved = advect(state, velocity[0, level], velocity[1, level], north_rows, south_rows, metric, cos_north, cos_south)
        weights.append((base_temp + moved[0]) * thickness[level])
        new_levels.append(smooth(moved, strength))
    below = jnp.zeros_like(surface)
    geo_levels = [None] * LEVELS
    for level in reversed(range(LEVELS)):
        geo_levels[level] = surface + below + 0.5 * weights[level]
        below = below + weights[level]
    new_fields = jnp.stack(new_levels, axis=1)
    geopotential = jnp.stack(geo_levels, axis=0)
    row_ids = jnp.arange(all_rows, dtype=jnp.int32)
    sort_key = jnp.where(row_owner >= 0, row_owner * all_rows + row_ids, all_rows * all_rows + row_ids)
    row_order = jnp.argsort(sort_key)[: all_rows // 2].astype(jnp.int32)
    polar_rows = jnp.take(new_fields, row_order, axis=2)
    return new_fields, geopotential, polar_rows
```

```python
import math

import jax
import jax.numpy as jnp
from jax import lax
from jax.experimental import pallas as pl
from jax.experimental.pallas import tpu as pltpu
from jax.sharding import PartitionSpec as P

PASSES = 8
MESH = pl.DeviceIdType.MESH
LANES = 128

courant_lon = 0.3
courant_lat = 0.3
diffuse_lon = 0.04
diffuse_lat = 0.08
base_temp = 3.0


def filtered(state, strength):
    width = state.shape[1]
    for _ in range(PASSES):
        slope = pltpu.roll(state, width - 1, 1) - state
        west = pltpu.roll(slope, 1, 1)
        east = pltpu.roll(slope, width - 1, 1)
        least = jnp.minimum(slope, jnp.minimum(west, east))
        most = jnp.maximum(slope, jnp.maximum(west, east))
        flux = strength * (slope - jnp.maximum(least, 0.0) - jnp.minimum(most, 0.0))
        state = state + flux - pltpu.roll(flux, 1, 1)
    return state


def make_kernel(lat_count, lev_count, nf, levels, rows, lons, segs):
    half = rows // 2
    slabs = nf * levels
    groups = rows // 8
    seg = lons // segs
    all_rows = rows * lat_count
    spacing = math.pi / all_rows
    shift = lat_count // 2
    quarter = lat_count // 4

    def kernel(
        fields, velocity, surface, thickness, row_owner,
        new_fields, geo, polar_rows,
        cells, wind, ground, halo, below, columns, packed, tables, owners, thick, slots,
        in_sem, wind_sem, small_sem, halo_send, halo_recv, col_send, col_recv, row_send, row_recv,
    ):
        me = lax.axis_index("lat")
        lev = lax.axis_index("lev")
        polar = (me < quarter) | (me >= lat_count - quarter)
        partner = lax.rem(me + shift, lat_count)

        def slab_of(step):
            return step // levels, levels - 1 - lax.rem(step, levels)

        def cell_copy(step):
            q, k = slab_of(step)
            return pltpu.make_async_copy(fields.at[q, k], cells.at[q, k], in_sem.at[step])

        def wind_copy(k, part):
            return pltpu.make_async_copy(velocity.at[part, k], wind.at[part, k], wind_sem.at[part, k])

        own_copy = pltpu.make_async_copy(row_owner, owners, small_sem.at[0])
        thick_copy = pltpu.make_async_copy(thickness, thick, small_sem.at[1])
        ground_copy = pltpu.make_async_copy(surface, ground, small_sem.at[2])

        barrier = pltpu.get_barrier_semaphore()
        for by in (shift, 1, lat_count - 1):
            pl.semaphore_signal(
                barrier, inc=1, device_id={"lat": lax.rem(me + by, lat_count)}, device_id_type=MESH
            )
        for by in range(1, lev_count):
            pl.semaphore_signal(
                barrier, inc=1, device_id={"lev": lax.rem(lev + by, lev_count)}, device_id_type=MESH
            )

        cell_copy(0).start()
        wind_copy(levels - 1, 0).start()
        wind_copy(levels - 1, 1).start()
        own_copy.start()
        thick_copy.start()
        for step in range(1, levels):
            cell_copy(step).start()
            wind_copy(levels - 1 - step, 0).start()
            wind_copy(levels - 1 - step, 1).start()
        for step in range(levels, slabs):
            cell_copy(step).start()
        ground_copy.start()

        row_index = me * rows + lax.broadcasted_iota(jnp.int32, (rows, LANES), 0)
        row_ids = row_index.astype(jnp.float32)
        lat_mid = -0.5 * math.pi + (row_ids + 0.5) * spacing
        cos_mid = jnp.cos(lat_mid)
        metric = 1.0 / jnp.maximum(cos_mid, 0.25)
        cos_north = jnp.cos(lat_mid + 0.5 * spacing)
        cos_south = jnp.cos(lat_mid - 0.5 * spacing)
        is_polar = (row_index < all_rows // 4) | (row_index >= all_rows - all_rows // 4)
        tables[0] = 0.5 * courant_lon * metric
        tables[1] = diffuse_lon * metric * metric
        tables[2] = diffuse_lat * metric * cos_north
        tables[3] = diffuse_lat * metric * cos_south
        tables[4] = jnp.where(
            is_polar, 0.05 + 0.2 * (1.0 - cos_mid / math.cos(0.25 * math.pi)), 0.0
        )

        own_copy.wait()
        thick_copy.wait()
        sent_from = [jnp.int32(0)] * half
        kept_from = [jnp.int32(0)] * half
        sent = jnp.int32(0)
        for row in range(rows):
            away = (owners[row] != me).astype(jnp.int32)
            kept = row - sent
            for slot in range(max(0, row - half), min(half, row + 1)):
                sent_from[slot] = jnp.where((away == 1) & (sent == slot), row, sent_from[slot])
                kept_from[slot] = jnp.where((away == 0) & (kept == slot), row, kept_from[slot])
            sent = sent + away
        for slot in range(half):
            slots[slot] = sent_from[slot]
            slots[half + slot] = kept_from[slot]

        pl.semaphore_wait(barrier, 3 + lev_count - 1)

        to_north = pltpu.make_async_remote_copy(
            src_ref=fields.at[:, :, rows - 1 : rows, :], dst_ref=halo.at[0],
            send_sem=halo_send.at[0], recv_sem=halo_recv.at[0],
            device_id={"lat": lax.rem(me + 1, lat_count)}, device_id_type=MESH,
        )
        to_south = pltpu.make_async_remote_copy(
            src_ref=fields.at[:, :, 0:1, :], dst_ref=halo.at[1],
            send_sem=halo_send.at[1], recv_sem=halo_recv.at[1],
            device_id={"lat": lax.rem(me + lat_count - 1, lat_count)}, device_id_type=MESH,
        )
        own_south = pltpu.make_async_copy(fields.at[:, :, 0:1, :], halo.at[0], halo_recv.at[0])
        own_north = pltpu.make_async_copy(fields.at[:, :, rows - 1 : rows, :], halo.at[1], halo_recv.at[1])
        first = me == 0
        last = me == lat_count - 1

        @pl.when(jnp.logical_not(last))
        def _():
            to_north.start()

        @pl.when(jnp.logical_not(first))
        def _():
            to_south.start()

        @pl.when(first)
        def _():
            own_south.start()

        @pl.when(last)
        def _():
            own_north.start()

        @pl.when(first)
        def _():
            own_south.wait()

        @pl.when(jnp.logical_not(first))
        def _():
            to_north.wait_recv()

        @pl.when(last)
        def _():
            own_north.wait()

        @pl.when(jnp.logical_not(last))
        def _():
            to_south.wait_recv()

        def row_copy(step, part):
            q, k = slab_of(step)
            cols = pl.ds(pl.multiple_of(part * seg, LANES), seg)
            return pltpu.make_async_remote_copy(
                src_ref=packed.at[q, k, :, cols], dst_ref=polar_rows.at[q, k, :, cols],
                send_sem=row_send.at[step, part], recv_sem=row_recv.at[step, part],
                device_id={"lat": partner}, device_id_type=MESH,
            )

        def col_copy(by):
            return pltpu.make_async_remote_copy(
                src_ref=below, dst_ref=columns.at[by - 1],
                send_sem=col_send.at[by - 1], recv_sem=col_recv.at[by - 1],
                device_id={"lev": lax.rem(lev + lev_count - by, lev_count)}, device_id_type=MESH,
            )

        blocks = lons // LANES
        per = seg // LANES

        def window(ref, lead, row, part):
            def at(block, n):
                return ref[(*lead, pl.ds(row, 8), pl.ds(pl.multiple_of(block * LANES, LANES), n * LANES))]

            return jnp.concatenate(
                [
                    at(lax.rem(part * per + blocks - 1, blocks), 1),
                    at(part * per, per),
                    at(lax.rem((part + 1) * per, blocks), 1),
                ],
                axis=1,
            )

        width = seg + 2 * LANES
        sub = lax.broadcasted_iota(jnp.int32, (8, width), 0)

        def spread(table, row):
            one = tables[table, pl.ds(row, 8), :]
            return jnp.concatenate([one] * (width // LANES), axis=1)

        def halo_window(side, q, k, part):
            def at(block, n):
                return halo[side, q, k, :, pl.ds(pl.multiple_of(block * LANES, LANES), n * LANES)]

            whole = jnp.concatenate(
                [
                    at(lax.rem(part * per + blocks - 1, blocks), 1),
                    at(part * per, per),
                    at(lax.rem((part + 1) * per, blocks), 1),
                ],
                axis=1,
            )
            return jnp.broadcast_to(whole, (8, width))

        def one_window(q, k, part, group):
            row = pl.multiple_of(group * 8, 8)
            cols = pl.ds(pl.multiple_of(part * seg, LANES), seg)
            state = window(cells, (q, k), row, part)
            above = pl.multiple_of(jnp.minimum(group + 1, groups - 1) * 8, 8)
            under = pl.multiple_of(jnp.maximum(group - 1, 0) * 8, 8)
            next_row = jnp.where(
                group == groups - 1,
                halo_window(1, q, k, part),
                pltpu.roll(window(cells, (q, k), above, part), 7, 0),
            )
            prev_row = jnp.where(
                group == 0,
                halo_window(0, q, k, part),
                pltpu.roll(window(cells, (q, k), under, part), 1, 0),
            )
            north = jnp.where(sub == 7, next_row, pltpu.roll(state, 7, 0))
            south = jnp.where(sub == 0, prev_row, pltpu.roll(state, 1, 0))
            wind_u = window(wind, (0, k), row, part)
            wind_v = window(wind, (1, k), row, part)
            east = pltpu.roll(state, width - 1, 1)
            west = pltpu.roll(state, 1, 1)
            result = state - spread(0, row) * wind_u * (east - west)
            result = result - (0.5 * courant_lat) * wind_v * (north - south)
            result = result + spread(1, row) * (east - 2.0 * state + west)
            result = result + spread(2, row) * (north - state) - spread(3, row) * (state - south)

            @pl.when(q == 0)
            def _():
                weight = (base_temp + result[:, LANES : LANES + seg]) * thick[k]
                so_far = jnp.where(k == levels - 1, 0.0, below[pl.ds(row, 8), cols])
                geo[k, pl.ds(row, 8), cols] = so_far + 0.5 * weight
                below[pl.ds(row, 8), cols] = so_far + weight

            @pl.when(jnp.logical_not(polar))
            def _():
                new_fields[q, k, pl.ds(row, 8), cols] = result[:, LANES : LANES + seg]

            @pl.when(polar)
            def _():
                smooth = filtered(result, spread(4, row))
                new_fields[q, k, pl.ds(row, 8), cols] = smooth[:, LANES : LANES + seg]

        def one_step(index, carry):
            step = index // segs
            part = lax.rem(index, segs)
            q, k = slab_of(step)
            cols = pl.ds(pl.multiple_of(part * seg, LANES), seg)

            @pl.when(part == 0)
            def _():
                cell_copy(step).wait()

            @pl.when((part == 0) & (step < levels))
            def _():
                wind_copy(k, 0).wait()
                wind_copy(k, 1).wait()

            def one_group(group, carry):
                one_window(q, k, part, group)
                return carry

            lax.fori_loop(0, groups, one_group, 0)

            @pl.when(polar)
            def _():
                for slot in range(half):
                    packed[q, k, slot : slot + 1, cols] = new_fields[q, k, pl.ds(slots[slot], 1), cols]
                row_copy(step, part).start()
                for slot in range(half):
                    polar_rows[q, k, slot : slot + 1, cols] = new_fields[
                        q, k, pl.ds(slots[half + slot], 1), cols
                    ]

            @pl.when((step == levels - 1) & (part == segs - 1))
            def _():
                for by in range(1, lev_count):
                    @pl.when(lev >= by)
                    def _():
                        col_copy(by).start()

            return carry

        lax.fori_loop(0, slabs * segs, one_step, 0)

        ground_copy.wait()
        for by in range(1, lev_count):
            @pl.when(lev + by < lev_count)
            def _():
                col_copy(by).wait_recv()

        def finish(index, carry):
            row = pl.multiple_of(index * 8, 8)
            outside = ground[pl.ds(row, 8), :]
            for by in range(1, lev_count):
                outside = outside + jnp.where(lev + by < lev_count, columns[by - 1, pl.ds(row, 8), :], 0.0)
            for k in range(levels):
                geo[k, pl.ds(row, 8), :] = geo[k, pl.ds(row, 8), :] + outside
            return carry

        lax.fori_loop(0, groups, finish, 0)

        for by in range(1, lev_count):
            @pl.when(lev >= by)
            def _():
                col_copy(by).wait_send()

        @pl.when(jnp.logical_not(last))
        def _():
            to_north.wait_send()

        @pl.when(jnp.logical_not(first))
        def _():
            to_south.wait_send()

        @pl.when(polar)
        def _():
            def drain(index, carry):
                row_copy(index // segs, lax.rem(index, segs)).wait_send()
                return carry

            lax.fori_loop(0, slabs * segs, drain, 0)

        @pl.when(jnp.logical_not(polar))
        def _():
            def arrive(index, carry):
                row_copy(index // segs, lax.rem(index, segs)).wait_recv()
                return carry

            lax.fori_loop(0, slabs * segs, arrive, 0)

    return kernel


def solution(mesh):
    lat_count, lev_count = mesh.shape["lat"], mesh.shape["lev"]
    segs = 4

    def local(fields, velocity, surface, thickness, row_owner):
        nf, levels, rows, lons = fields.shape
        half = rows // 2
        any_spec = pl.BlockSpec(memory_space=pl.ANY)
        vmem_spec = pl.BlockSpec(memory_space=pltpu.VMEM)
        dma = pltpu.SemaphoreType.DMA
        f32 = jnp.float32
        return pl.pallas_call(
            make_kernel(lat_count, lev_count, nf, levels, rows, lons, segs),
            out_shape=(
                pltpu.VMEM((nf, levels, rows, lons), f32),
                pltpu.VMEM((levels, rows, lons), f32),
                pltpu.VMEM((nf, levels, half, lons), f32),
            ),
            in_specs=[any_spec] * 5,
            out_specs=[vmem_spec] * 3,
            scratch_shapes=[
                pltpu.VMEM((nf, levels, rows, lons), f32),
                pltpu.VMEM((2, levels, rows, lons), f32),
                pltpu.VMEM((rows, lons), f32),
                pltpu.VMEM((2, nf, levels, 1, lons), f32),
                pltpu.VMEM((rows, lons), f32),
                pltpu.VMEM((lev_count - 1, rows, lons), f32),
                pltpu.VMEM((nf, levels, half, lons), f32),
                pltpu.VMEM((5, rows, LANES), f32),
                pltpu.SMEM((rows,), jnp.int32),
                pltpu.SMEM((levels,), f32),
                pltpu.SMEM((rows,), jnp.int32),
                dma((nf * levels,)),
                dma((2, levels)),
                dma((3,)),
                dma((2,)),
                dma((2,)),
                dma((lev_count - 1,)),
                dma((lev_count - 1,)),
                dma((nf * levels, segs)),
                dma((nf * levels, segs)),
            ],
            compiler_params=pltpu.CompilerParams(
                collective_id=0, has_side_effects=True, vmem_limit_bytes=40 * 1024 * 1024
            ),
            name="step",
        )(fields, velocity, surface, thickness, row_owner)

    in_specs = (
        P(None, "lev", "lat", None),
        P(None, "lev", "lat", None),
        P("lat", None),
        P("lev"),
        P("lat"),
    )
    out_specs = (P(None, "lev", "lat", None), P("lev", "lat", None), P(None, "lev", "lat", None))
    return jax.shard_map(local, mesh=mesh, in_specs=in_specs, out_specs=out_specs, check_vma=False)
```

```python
import math

import jax
import jax.numpy as jnp
from jax import lax
from jax.experimental import pallas as pl
from jax.experimental.pallas import tpu as pltpu
from jax.sharding import PartitionSpec as P

PASSES = 8
PAD = 2 * PASSES
SLACK = 32
STEPS = 68
LANES = 128
SUBS = 8
CHUNK = 512
MESH = pl.DeviceIdType.MESH

courant_lon = 0.3
courant_lat = 0.3
diffuse_lon = 0.04
diffuse_lat = 0.08
base_temp = 3.0


def strength_of(row_ids, all_rows):
    cos_mid = jnp.cos(-0.5 * math.pi + (row_ids + 0.5) * (math.pi / all_rows))
    polar = (row_ids < all_rows // 4) | (row_ids >= all_rows - all_rows // 4)
    return jnp.where(polar, 0.05 + 0.2 * (1.0 - cos_mid / math.cos(0.25 * math.pi)), 0.0)


def make_kernel(lat_count, lev_count, nf, levels, rows, lons):
    half = rows // 2
    slabs = nf * levels
    groups = rows // SUBS
    all_rows = rows * lat_count
    spacing = math.pi / all_rows
    shift = lat_count // 2
    quarter = lat_count // 4
    blocks = lons // LANES
    per = CHUNK // LANES
    chunks = lons // CHUNK
    segment = lons // SUBS
    per_segment = segment // LANES
    length = segment + 2 * PAD + SLACK
    last_q = nf - 1

    def kernel(
        fields, velocity, surface, thickness, row_owner,
        new_fields, geo, polar_rows,
        cells, wind, ground, halo, below, columns, packed, landed, front, back,
        tables, factor, factor_out, owners, thick, slots,
        in_sem, wind_sem, small_sem, halo_send, halo_recv, col_send, col_recv, row_send, row_recv,
        factor_sem,
    ):
        me = lax.axis_index("lat")
        lev = lax.axis_index("lev")
        polar = (me < quarter) | (me >= lat_count - quarter)
        plain = jnp.logical_not(polar)
        partner = lax.rem(me + shift, lat_count)

        def cell_copy(q, k):
            return pltpu.make_async_copy(fields.at[q, k], cells.at[q, k], in_sem.at[q, k])

        def wind_copy(k, part):
            return pltpu.make_async_copy(velocity.at[part, k], wind.at[part, k], wind_sem.at[part, k])

        own_copy = pltpu.make_async_copy(row_owner, owners, small_sem.at[0])
        thick_copy = pltpu.make_async_copy(thickness, thick, small_sem.at[1])
        ground_copy = pltpu.make_async_copy(surface, ground, small_sem.at[2])

        barrier = pltpu.get_barrier_semaphore()
        for by in (shift, 1, lat_count - 1):
            pl.semaphore_signal(
                barrier, inc=1, device_id={"lat": lax.rem(me + by, lat_count)}, device_id_type=MESH
            )
        for by in range(1, lev_count):
            pl.semaphore_signal(
                barrier, inc=1, device_id={"lev": lax.rem(lev + by, lev_count)}, device_id_type=MESH
            )

        for q in range(nf):
            for k in reversed(range(levels)):
                cell_copy(q, k).start()
                if q == 0:
                    wind_copy(k, 0).start()
                    wind_copy(k, 1).start()
                    if k == levels - 1:
                        own_copy.start()
                        thick_copy.start()
        ground_copy.start()

        row_ids = (me * rows + lax.broadcasted_iota(jnp.int32, (rows, LANES), 0)).astype(jnp.float32)
        lat_mid = -0.5 * math.pi + (row_ids + 0.5) * spacing
        metric = 1.0 / jnp.maximum(jnp.cos(lat_mid), 0.25)
        to_north = diffuse_lat * metric * jnp.cos(lat_mid + 0.5 * spacing)
        to_south = diffuse_lat * metric * jnp.cos(lat_mid - 0.5 * spacing)
        to_side = diffuse_lon * metric * metric
        tables[0] = 0.5 * courant_lon * metric
        tables[1] = to_side
        tables[2] = to_north
        tables[3] = to_south
        tables[4] = 1.0 - 2.0 * to_side - to_north - to_south

        lane = lax.broadcasted_iota(jnp.int32, (SUBS, LANES), 1)
        for place in range(SLACK):
            at = (segment + 2 * PAD + place) * SUBS
            front[at : at + SUBS, :] = jnp.zeros((SUBS, LANES), jnp.float32)

        own_copy.wait()
        thick_copy.wait()
        sent_from = [jnp.int32(0)] * half
        kept_from = [jnp.int32(0)] * half
        sent = jnp.int32(0)
        for row in range(rows):
            away = (owners[row] != me).astype(jnp.int32)
            kept = row - sent
            for slot in range(max(0, row - half), min(half, row + 1)):
                sent_from[slot] = jnp.where((away == 1) & (sent == slot), row, sent_from[slot])
                kept_from[slot] = jnp.where((away == 0) & (kept == slot), row, kept_from[slot])
            sent = sent + away
        for slot in range(half):
            slots[slot] = sent_from[slot]
            slots[half + slot] = kept_from[slot]

        @pl.when(polar)
        def _():
            here = lax.rem(lane, rows)
            away = jnp.zeros((SUBS, LANES), jnp.int32)
            slot_of = lax.rem(lane, half)
            for slot in range(half):
                away = jnp.where(slot_of == slot, slots[slot], away)
            factor[...] = strength_of((me * rows + here).astype(jnp.float32), all_rows)
            factor_out[...] = strength_of((me * rows + away).astype(jnp.float32), all_rows)

        pl.semaphore_wait(barrier, 3 + lev_count - 1)

        north_copy = pltpu.make_async_remote_copy(
            src_ref=fields.at[:, :, rows - 1 : rows, :], dst_ref=halo.at[0],
            send_sem=halo_send.at[0], recv_sem=halo_recv.at[0],
            device_id={"lat": lax.rem(me + 1, lat_count)}, device_id_type=MESH,
        )
        south_copy = pltpu.make_async_remote_copy(
            src_ref=fields.at[:, :, 0:1, :], dst_ref=halo.at[1],
            send_sem=halo_send.at[1], recv_sem=halo_recv.at[1],
            device_id={"lat": lax.rem(me + lat_count - 1, lat_count)}, device_id_type=MESH,
        )
        own_south = pltpu.make_async_copy(fields.at[:, :, 0:1, :], halo.at[0], halo_recv.at[0])
        own_north = pltpu.make_async_copy(fields.at[:, :, rows - 1 : rows, :], halo.at[1], halo_recv.at[1])
        first = me == 0
        last = me == lat_count - 1

        @pl.when(jnp.logical_not(last))
        def _():
            north_copy.start()

        @pl.when(jnp.logical_not(first))
        def _():
            south_copy.start()

        @pl.when(first)
        def _():
            own_south.start()

        @pl.when(last)
        def _():
            own_north.start()

        factor_copy = pltpu.make_async_remote_copy(
            src_ref=factor_out, dst_ref=factor, send_sem=factor_sem.at[0], recv_sem=factor_sem.at[1],
            device_id={"lat": partner}, device_id_type=MESH,
        )

        def early_copy(q, k):
            return pltpu.make_async_remote_copy(
                src_ref=packed.at[q, k], dst_ref=landed.at[q, k],
                send_sem=row_send.at[q, k], recv_sem=row_recv.at[q, k],
                device_id={"lat": partner}, device_id_type=MESH,
            )

        def late_copy(k):
            return pltpu.make_async_remote_copy(
                src_ref=packed.at[last_q, k], dst_ref=polar_rows.at[last_q, k],
                send_sem=row_send.at[last_q, k], recv_sem=row_recv.at[last_q, k],
                device_id={"lat": partner}, device_id_type=MESH,
            )

        def col_copy(by):
            return pltpu.make_async_remote_copy(
                src_ref=below, dst_ref=columns.at[by - 1],
                send_sem=col_send.at[by - 1], recv_sem=col_recv.at[by - 1],
                device_id={"lev": lax.rem(lev + lev_count - by, lev_count)}, device_id_type=MESH,
            )

        @pl.when(polar)
        def _():
            factor_copy.start()

        @pl.when(first)
        def _():
            own_south.wait()

        @pl.when(jnp.logical_not(first))
        def _():
            north_copy.wait_recv()

        @pl.when(last)
        def _():
            own_north.wait()

        @pl.when(jnp.logical_not(last))
        def _():
            south_copy.wait_recv()

        sub = lax.broadcasted_iota(jnp.int32, (SUBS, CHUNK), 0)

        def advect_chunk(q, k, part):
            cols = pl.ds(pl.multiple_of(part * CHUNK, LANES), CHUNK)
            left = pl.ds(pl.multiple_of(lax.rem(part * per + blocks - 1, blocks) * LANES, LANES), LANES)
            right = pl.ds(pl.multiple_of(lax.rem((part + 1) * per, blocks) * LANES, LANES), LANES)

            def spread(table, group):
                one = tables[table, group * SUBS : (group + 1) * SUBS, :]
                return jnp.concatenate([one] * per, axis=1)

            state = [cells[q, k, g * SUBS : (g + 1) * SUBS, cols] for g in range(groups)]
            up = [pltpu.roll(one, SUBS - 1, 0) for one in state]
            up.append(jnp.broadcast_to(halo[1, q, k, :, cols], (SUBS, CHUNK)))
            down = [jnp.broadcast_to(halo[0, q, k, :, cols], (SUBS, CHUNK))]
            down += [pltpu.roll(one, 1, 0) for one in state]
            for g in range(groups):
                span = pl.ds(g * SUBS, SUBS)
                wide = CHUNK + LANES
                east = pltpu.roll(jnp.concatenate([state[g], cells[q, k, span, right]], axis=1), wide - 1, 1)
                west = pltpu.roll(jnp.concatenate([cells[q, k, span, left], state[g]], axis=1), 1, 1)
                east, west = east[:, :CHUNK], west[:, LANES:]
                north = jnp.where(sub == SUBS - 1, up[g + 1], up[g])
                south = jnp.where(sub == 0, down[g], down[g + 1])
                along = spread(0, g) * wind[0, k, span, cols]
                across = (0.5 * courant_lat) * wind[1, k, span, cols]
                side = spread(1, g)
                result = (
                    spread(4, g) * state[g]
                    + ((side - along) * east + (side + along) * west)
                    + ((spread(2, g) - across) * north + (spread(3, g) + across) * south)
                )
                new_fields[q, k, span, cols] = result
                if isinstance(q, int) and q == 0:
                    weight = (base_temp + result) * thick[k]
                    so_far = jnp.where(k == levels - 1, 0.0, below[span, cols])
                    geo[k, span, cols] = so_far + 0.5 * weight
                    below[span, cols] = so_far + weight

        def advect_level(q, k):
            def one(part, carry):
                advect_chunk(q, k, part)
                return carry

            lax.fori_loop(0, chunks, one, 0)

        def pack(q, k):
            for slot in range(half):
                packed[q, k, slot : slot + 1, :] = new_fields[q, k, pl.ds(slots[slot], 1), :]

        def keep(q, k):
            for slot in range(half):
                polar_rows[q, k, slot : slot + 1, :] = new_fields[q, k, pl.ds(slots[half + slot], 1), :]

        def first_field(index, carry):
            k = levels - 1 - index
            cell_copy(0, k).wait()
            wind_copy(k, 0).wait()
            wind_copy(k, 1).wait()
            advect_level(0, k)

            @pl.when(polar)
            def _():
                pack(0, k)
                early_copy(0, k).start()

            return carry

        lax.fori_loop(0, levels, first_field, 0)

        for by in range(1, lev_count):
            @pl.when(lev >= by)
            def _():
                col_copy(by).start()

        def next_field(index, carry):
            q = 1 + index // levels
            k = levels - 1 - lax.rem(index, levels)
            cell_copy(q, k).wait()
            advect_level(q, k)

            @pl.when(polar & (q < last_q))
            def _():
                pack(q, k)
                early_copy(q, k).start()

            return carry

        lax.fori_loop(0, slabs - levels, next_field, 0)

        def place_of(block):
            return lax.rem(block, per_segment) * LANES + PAD, block // per_segment

        def run(place):
            return pl.ds(pl.multiple_of(place * SUBS, SUBS), SUBS)

        def put_block(block, values):
            start, which = place_of(block)
            turned = values.T
            for v in range(LANES // SUBS):
                front[pl.ds((start + SUBS * v) * SUBS + which, SUBS, stride=SUBS), :] = turned[
                    SUBS * v : SUBS * (v + 1), :
                ]

        def get_block(block):
            start, which = place_of(block)
            return jnp.concatenate(
                [
                    front[pl.ds((start + SUBS * v) * SUBS + which, SUBS, stride=SUBS), :]
                    for v in range(LANES // SUBS)
                ],
                axis=0,
            ).T

        def cols_of(block):
            return pl.ds(pl.multiple_of(block * LANES, LANES), LANES)

        def one_pass(source, target, start, strength):
            def flux_of(west, slope, east):
                least = jnp.minimum(jnp.maximum(west, east), 0.0)
                most = jnp.maximum(jnp.minimum(west, east), 0.0)
                return strength * (slope - jnp.minimum(jnp.maximum(slope, least), most))

            def steps(index, state):
                cell, ahead, west, slope, inflow = state
                base = start + index * STEPS
                for j in range(STEPS):
                    beyond = source[run(base + j + 2), :]
                    east = beyond - ahead
                    outflow = flux_of(west, slope, east)
                    target[run(base + j), :] = cell + (outflow - inflow)
                    cell, ahead, west, slope, inflow = ahead, beyond, slope, east, outflow
                return cell, ahead, west, slope, inflow

            near = [source[run(start - 2 + j), :] for j in range(4)]
            slopes = [near[j + 1] - near[j] for j in range(3)]
            inflow = flux_of(slopes[0], slopes[1], slopes[2])
            lax.fori_loop(
                0, (length - SLACK) // STEPS, steps, (near[2], near[3], slopes[1], slopes[2], inflow)
            )

        def all_passes():
            for j in range(PAD):
                front[j * SUBS : (j + 1) * SUBS, :] = pltpu.roll(
                    front[(segment + j) * SUBS : (segment + j + 1) * SUBS, :], 1, 0
                )
                end = (PAD + segment + j) * SUBS
                front[end : end + SUBS, :] = pltpu.roll(
                    front[(PAD + j) * SUBS : (PAD + j + 1) * SUBS, :], SUBS - 1, 0
                )
            strength = factor[...]

            def pair(index, carry):
                one_pass(front, back, 2 + 4 * index, strength)
                one_pass(back, front, 4 + 4 * index, strength)
                return carry

            lax.fori_loop(0, PASSES // 2, pair, 0)

        @pl.when(plain)
        def _():
            factor_copy.wait_recv()

        def job(index, carry):
            q = lax.rem(index + last_q, nf)

            @pl.when(polar)
            def _():
                def fill(block, carry):
                    values = new_fields[q, :, :, cols_of(block)]
                    put_block(block, values.reshape(LANES, LANES))
                    return carry

                lax.fori_loop(0, blocks, fill, 0)

            @pl.when(plain & (index < last_q))
            def _():
                def heard(k, carry):
                    early_copy(index, levels - 1 - k).wait_recv()
                    return carry

                lax.fori_loop(0, levels, heard, 0)

                def fill(block, carry):
                    values = landed[index, :, :, cols_of(block)].reshape(levels * half, LANES)
                    put_block(block, jnp.concatenate([values, values], axis=0))
                    return carry

                lax.fori_loop(0, blocks, fill, 0)

            @pl.when(polar | (index < last_q))
            def _():
                all_passes()

            @pl.when(polar)
            def _():
                def spill(block, carry):
                    new_fields[q, :, :, cols_of(block)] = get_block(block).reshape(levels, rows, LANES)
                    return carry

                lax.fori_loop(0, blocks, spill, 0)

                @pl.when(index == 0)
                def _():
                    def send(k, carry):
                        pack(last_q, k)
                        late_copy(k).start()
                        return carry

                    lax.fori_loop(0, levels, send, 0)

                def hold(k, carry):
                    keep(q, k)
                    return carry

                lax.fori_loop(0, levels, hold, 0)

            @pl.when(plain & (index < last_q))
            def _():
                def spill(block, carry):
                    values = get_block(block)[: levels * half, :]
                    polar_rows[index, :, :, cols_of(block)] = values.reshape(levels, half, LANES)
                    return carry

                lax.fori_loop(0, blocks, spill, 0)

            return carry

        lax.fori_loop(0, nf, job, 0)

        ground_copy.wait()
        for by in range(1, lev_count):
            @pl.when(lev + by < lev_count)
            def _():
                col_copy(by).wait_recv()

        def finish(index, carry):
            span = pl.ds(pl.multiple_of(index * SUBS, SUBS), SUBS)
            outside = ground[span, :]
            for by in range(1, lev_count):
                outside = outside + jnp.where(lev + by < lev_count, columns[by - 1, span, :], 0.0)
            for k in range(levels):
                geo[k, span, :] = geo[k, span, :] + outside
            return carry

        lax.fori_loop(0, groups, finish, 0)

        for by in range(1, lev_count):
            @pl.when(lev >= by)
            def _():
                col_copy(by).wait_send()

        @pl.when(jnp.logical_not(last))
        def _():
            north_copy.wait_send()

        @pl.when(jnp.logical_not(first))
        def _():
            south_copy.wait_send()

        @pl.when(polar)
        def _():
            factor_copy.wait_send()
            for q in range(last_q):
                for k in range(levels):
                    early_copy(q, k).wait_send()
            for k in range(levels):
                late_copy(k).wait_send()

        @pl.when(plain)
        def _():
            for k in range(levels):
                late_copy(k).wait_recv()

    return kernel


def write_out(new_fields, geo, polar_rows, new_fields_out, geo_out, polar_rows_out, sem):
    copies = [
        pltpu.make_async_copy(new_fields, new_fields_out, sem.at[0]),
        pltpu.make_async_copy(geo, geo_out, sem.at[1]),
        pltpu.make_async_copy(polar_rows, polar_rows_out, sem.at[2]),
    ]
    for copy in copies:
        copy.start()
    for copy in copies:
        copy.wait()


def solution(mesh):
    lat_count, lev_count = mesh.shape["lat"], mesh.shape["lev"]

    def local(fields, velocity, surface, thickness, row_owner):
        nf, levels, rows, lons = fields.shape
        half = rows // 2
        length = lons // SUBS + 2 * PAD + SLACK
        hbm_spec = pl.BlockSpec(memory_space=pltpu.HBM)
        vmem_spec = pl.BlockSpec(memory_space=pltpu.VMEM)
        dma = pltpu.SemaphoreType.DMA
        f32 = jnp.float32
        shapes = ((nf, levels, rows, lons), (levels, rows, lons), (nf, levels, half, lons))
        held = pl.pallas_call(
            make_kernel(lat_count, lev_count, nf, levels, rows, lons),
            out_shape=tuple(pltpu.VMEM(shape, f32) for shape in shapes),
            in_specs=[hbm_spec] * 5,
            out_specs=[vmem_spec] * 3,
            scratch_shapes=[
                pltpu.VMEM((nf, levels, rows, lons), f32),
                pltpu.VMEM((2, levels, rows, lons), f32),
                pltpu.VMEM((rows, lons), f32),
                pltpu.VMEM((2, nf, levels, 1, lons), f32),
                pltpu.VMEM((rows, lons), f32),
                pltpu.VMEM((lev_count - 1, rows, lons), f32),
                pltpu.VMEM((nf, levels, half, lons), f32),
                pltpu.VMEM((nf - 1, levels, half, lons), f32),
                pltpu.VMEM((length * SUBS, LANES), f32),
                pltpu.VMEM((length * SUBS, LANES), f32),
                pltpu.VMEM((5, rows, LANES), f32),
                pltpu.VMEM((SUBS, LANES), f32),
                pltpu.VMEM((SUBS, LANES), f32),
                pltpu.SMEM((rows,), jnp.int32),
                pltpu.SMEM((levels,), f32),
                pltpu.SMEM((rows,), jnp.int32),
                dma((nf, levels)),
                dma((2, levels)),
                dma((3,)),
                dma((2,)),
                dma((2,)),
                dma((lev_count - 1,)),
                dma((lev_count - 1,)),
                dma((nf, levels)),
                dma((nf, levels)),
                dma((2,)),
            ],
            compiler_params=pltpu.CompilerParams(
                collective_id=0, has_side_effects=True, vmem_limit_bytes=40 * 1024 * 1024
            ),
            name="step",
        )(fields, velocity, surface, thickness, row_owner)
        return pl.pallas_call(
            write_out,
            out_shape=tuple(jax.ShapeDtypeStruct(shape, f32) for shape in shapes),
            in_specs=[pl.BlockSpec(memory_space=pl.ANY)] * 3,
            out_specs=[hbm_spec] * 3,
            scratch_shapes=[dma((3,))],
            compiler_params=pltpu.CompilerParams(vmem_limit_bytes=1024 * 1024),
            name="write",
        )(*held)

    in_specs = (
        P(None, "lev", "lat", None),
        P(None, "lev", "lat", None),
        P("lat", None),
        P("lev"),
        P("lat"),
    )
    out_specs = (P(None, "lev", "lat", None), P("lev", "lat", None), P(None, "lev", "lat", None))
    return jax.shard_map(local, mesh=mesh, in_specs=in_specs, out_specs=out_specs, check_vma=False)
```

```python
import math

import jax
import jax.numpy as jnp
from jax import lax
from jax.experimental import pallas as pl
from jax.experimental.pallas import tpu as pltpu
from jax.sharding import PartitionSpec as P

PASSES = 8
PAD = 2 * PASSES
SLACK = 32
STEPS = 68
LANES = 128
SUBS = 8
CHUNK = 512
UNROLL = 8
MESH = pl.DeviceIdType.MESH

courant_lon = 0.3
courant_lat = 0.3
diffuse_lon = 0.04
diffuse_lat = 0.08
base_temp = 3.0


def strength_of(row_ids, all_rows):
    cos_mid = jnp.cos(-0.5 * math.pi + (row_ids + 0.5) * (math.pi / all_rows))
    polar = (row_ids < all_rows // 4) | (row_ids >= all_rows - all_rows // 4)
    return jnp.where(polar, 0.05 + 0.2 * (1.0 - cos_mid / math.cos(0.25 * math.pi)), 0.0)


def make_kernel(lat_count, lev_count, nf, levels, rows, lons):
    half = rows // 2
    slabs = nf * levels
    groups = rows // SUBS
    all_rows = rows * lat_count
    spacing = math.pi / all_rows
    shift = lat_count // 2
    quarter = lat_count // 4
    blocks = lons // LANES
    per = CHUNK // LANES
    chunks = lons // CHUNK
    segment = lons // SUBS
    per_segment = segment // LANES
    length = segment + 2 * PAD + SLACK
    last_q = nf - 1
    order = list(range(1, half - 1)) + [0, half - 1]

    def kernel(
        fields, velocity, surface, thickness, row_owner,
        new_fields, geo, polar_rows,
        cells, wind, ground, halo, below, columns, packed, landed, front, back,
        tables, factor, factor_out, owners, thick, slots,
        in_sem, wind_sem, small_sem, halo_send, halo_recv, col_send, col_recv, early_send,
        early_recv, late_send, late_recv, factor_sem,
    ):
        me = lax.axis_index("lat")
        lev = lax.axis_index("lev")
        polar = (me < quarter) | (me >= lat_count - quarter)
        plain = jnp.logical_not(polar)
        partner = lax.rem(me + shift, lat_count)

        def cell_copy(q, k):
            return pltpu.make_async_copy(fields.at[q, k], cells.at[q, k], in_sem.at[q, k])

        def wind_copy(k, part):
            return pltpu.make_async_copy(velocity.at[part, k], wind.at[part, k], wind_sem.at[part, k])

        own_copy = pltpu.make_async_copy(row_owner, owners, small_sem.at[0])
        thick_copy = pltpu.make_async_copy(thickness, thick, small_sem.at[1])
        ground_copy = pltpu.make_async_copy(surface, ground, small_sem.at[2])

        barrier = pltpu.get_barrier_semaphore()
        for by in (shift, 1, lat_count - 1):
            pl.semaphore_signal(
                barrier, inc=1, device_id={"lat": lax.rem(me + by, lat_count)}, device_id_type=MESH
            )
        for by in range(1, lev_count):
            pl.semaphore_signal(
                barrier, inc=1, device_id={"lev": lax.rem(lev + by, lev_count)}, device_id_type=MESH
            )

        for q in range(nf):
            for k in reversed(range(levels)):
                cell_copy(q, k).start()
                if q == 0:
                    wind_copy(k, 0).start()
                    wind_copy(k, 1).start()
                    if k == levels - 1:
                        own_copy.start()
                        thick_copy.start()
        ground_copy.start()

        row_ids = (me * rows + lax.broadcasted_iota(jnp.int32, (rows, LANES), 0)).astype(jnp.float32)
        lat_mid = -0.5 * math.pi + (row_ids + 0.5) * spacing
        metric = 1.0 / jnp.maximum(jnp.cos(lat_mid), 0.25)
        to_north = diffuse_lat * metric * jnp.cos(lat_mid + 0.5 * spacing)
        to_south = diffuse_lat * metric * jnp.cos(lat_mid - 0.5 * spacing)
        to_side = diffuse_lon * metric * metric
        tables[0] = 0.5 * courant_lon * metric
        tables[1] = to_side
        tables[2] = to_north
        tables[3] = to_south
        tables[4] = 1.0 - 2.0 * to_side - to_north - to_south

        lane = lax.broadcasted_iota(jnp.int32, (SUBS, LANES), 1)
        for place in range(SLACK):
            at = (segment + 2 * PAD + place) * SUBS
            front[at : at + SUBS, :] = jnp.zeros((SUBS, LANES), jnp.float32)

        own_copy.wait()
        thick_copy.wait()
        sent, kept = [], []
        for row in range(rows):
            away = (owners[row] != me).astype(jnp.int32)
            sent.append(away + (sent[-1] if row else 0))
            kept.append(row + 1 - sent[-1])

        def fill_slots(counts, base):
            for slot in range(half):
                place = jnp.int32(slot)
                for row in range(slot, slot + half):
                    place = place + (counts[row] <= slot).astype(jnp.int32)
                slots[base + slot] = place

        fill_slots(sent, 0)

        north_copy = pltpu.make_async_remote_copy(
            src_ref=fields.at[:, :, rows - 1 : rows, :], dst_ref=halo.at[0],
            send_sem=halo_send.at[0], recv_sem=halo_recv.at[0],
            device_id={"lat": lax.rem(me + 1, lat_count)}, device_id_type=MESH,
        )
        south_copy = pltpu.make_async_remote_copy(
            src_ref=fields.at[:, :, 0:1, :], dst_ref=halo.at[1],
            send_sem=halo_send.at[1], recv_sem=halo_recv.at[1],
            device_id={"lat": lax.rem(me + lat_count - 1, lat_count)}, device_id_type=MESH,
        )
        own_south = pltpu.make_async_copy(fields.at[:, :, 0:1, :], halo.at[0], halo_recv.at[0])
        own_north = pltpu.make_async_copy(fields.at[:, :, rows - 1 : rows, :], halo.at[1], halo_recv.at[1])
        first = me == 0
        last = me == lat_count - 1

        factor_copy = pltpu.make_async_remote_copy(
            src_ref=factor_out, dst_ref=factor, send_sem=factor_sem.at[0], recv_sem=factor_sem.at[1],
            device_id={"lat": partner}, device_id_type=MESH,
        )

        def early_copy(q, k, part):
            span = pl.ds(part * SUBS, SUBS)
            return pltpu.make_async_remote_copy(
                src_ref=packed.at[q, k, span], dst_ref=landed.at[q, k, span],
                send_sem=early_send.at[q, k, part], recv_sem=early_recv.at[q, k, part],
                device_id={"lat": partner}, device_id_type=MESH,
            )

        def late_copy(k):
            return pltpu.make_async_remote_copy(
                src_ref=packed.at[last_q, k], dst_ref=polar_rows.at[last_q, k],
                send_sem=late_send.at[k], recv_sem=late_recv.at[k],
                device_id={"lat": partner}, device_id_type=MESH,
            )

        def col_copy(by):
            return pltpu.make_async_remote_copy(
                src_ref=below, dst_ref=columns.at[by - 1],
                send_sem=col_send.at[by - 1], recv_sem=col_recv.at[by - 1],
                device_id={"lev": lax.rem(lev + lev_count - by, lev_count)}, device_id_type=MESH,
            )

        sub = lax.broadcasted_iota(jnp.int32, (SUBS, CHUNK), 0)

        def advect_chunk(q, k, part, edges):
            cols = pl.ds(pl.multiple_of(part * CHUNK, LANES), CHUNK)
            left = pl.ds(pl.multiple_of(lax.rem(part * per + blocks - 1, blocks) * LANES, LANES), LANES)
            right = pl.ds(pl.multiple_of(lax.rem((part + 1) * per, blocks) * LANES, LANES), LANES)

            def spread(table, group):
                one = tables[table, group * SUBS : (group + 1) * SUBS, :]
                return jnp.concatenate([one] * per, axis=1)

            state = [cells[q, k, g * SUBS : (g + 1) * SUBS, cols] for g in range(groups)]
            up = [pltpu.roll(one, SUBS - 1, 0) for one in state]
            if edges:
                up.append(jnp.broadcast_to(halo[1, q, k, :, cols], (SUBS, CHUNK)))
                down = [jnp.broadcast_to(halo[0, q, k, :, cols], (SUBS, CHUNK))]
            else:
                up.append(state[groups - 1])
                down = [state[0]]
            down += [pltpu.roll(one, 1, 0) for one in state]
            for g in range(groups):
                span = pl.ds(g * SUBS, SUBS)
                wide = CHUNK + LANES
                east = pltpu.roll(jnp.concatenate([state[g], cells[q, k, span, right]], axis=1), wide - 1, 1)
                west = pltpu.roll(jnp.concatenate([cells[q, k, span, left], state[g]], axis=1), 1, 1)
                east, west = east[:, :CHUNK], west[:, LANES:]
                north = jnp.where(sub == SUBS - 1, up[g + 1], up[g])
                south = jnp.where(sub == 0, down[g], down[g + 1])
                along = spread(0, g) * wind[0, k, span, cols]
                across = (0.5 * courant_lat) * wind[1, k, span, cols]
                side = spread(1, g)
                result = (
                    spread(4, g) * state[g]
                    + ((side - along) * east + (side + along) * west)
                    + ((spread(2, g) - across) * north + (spread(3, g) + across) * south)
                )
                new_fields[q, k, span, cols] = result

        def advect_level(q, k, edges):
            def one(part, carry):
                advect_chunk(q, k, part, edges)
                return carry

            lax.fori_loop(0, chunks, one, 0)

        def pack(q, k, chosen, start=0):
            for place, slot in enumerate(chosen):
                packed[q, k, start + place : start + place + 1, :] = new_fields[
                    q, k, pl.ds(slots[slot], 1), :
                ]

        def keep(q, k):
            for slot in range(half):
                polar_rows[q, k, slot : slot + 1, :] = new_fields[q, k, pl.ds(slots[half + slot], 1), :]

        def first_level(k):
            cell_copy(0, k).wait()
            wind_copy(k, 0).wait()
            wind_copy(k, 1).wait()
            advect_level(0, k, False)

            @pl.when(polar)
            def _():
                pack(0, k, order[:SUBS])

        first_level(levels - 1)
        pl.semaphore_wait(barrier, 3 + lev_count - 1)

        @pl.when(polar)
        def _():
            early_copy(0, levels - 1, 0).start()

        @pl.when(jnp.logical_not(last))
        def _():
            north_copy.start()

        @pl.when(jnp.logical_not(first))
        def _():
            south_copy.start()

        @pl.when(first)
        def _():
            own_south.start()

        @pl.when(last)
        def _():
            own_north.start()

        def other_levels(index, carry):
            k = levels - 2 - index
            first_level(k)

            @pl.when(polar)
            def _():
                early_copy(0, k, 0).start()

            return carry

        lax.fori_loop(0, levels - 1, other_levels, 0)

        @pl.when(polar)
        def _():
            here = lax.rem(lane, rows)
            away = jnp.zeros((SUBS, LANES), jnp.int32)
            slot_of = lax.rem(lane, half)
            for place, slot in enumerate(order):
                away = jnp.where(slot_of == place, slots[slot], away)
            factor[...] = strength_of((me * rows + here).astype(jnp.float32), all_rows)
            factor_out[...] = strength_of((me * rows + away).astype(jnp.float32), all_rows)

        @pl.when(polar)
        def _():
            factor_copy.start()

        @pl.when(first)
        def _():
            own_south.wait()

        @pl.when(jnp.logical_not(first))
        def _():
            north_copy.wait_recv()

        @pl.when(last)
        def _():
            own_north.wait()

        @pl.when(jnp.logical_not(last))
        def _():
            south_copy.wait_recv()

        def mend_edges(k, part):
            cols = pl.ds(pl.multiple_of(part * CHUNK, LANES), CHUNK)
            for side, group, line, sign in ((0, 0, 0, 1.0), (1, groups - 1, SUBS - 1, -1.0)):
                span = pl.ds(group * SUBS, SUBS)
                table = tables[3 - side, span, :]
                weight = (
                    jnp.concatenate([table] * per, axis=1)
                    + (sign * 0.5 * courant_lat) * wind[1, k, span, cols]
                )
                beyond = jnp.broadcast_to(halo[side, 0, k, :, cols], (SUBS, CHUNK))
                change = weight * (beyond - cells[0, k, span, cols])
                new_fields[0, k, span, cols] = new_fields[0, k, span, cols] + jnp.where(
                    sub == line, change, 0.0
                )

        def mend_level(index, carry):
            k = levels - 1 - index

            def one(part, carry):
                mend_edges(k, part)
                return carry

            lax.fori_loop(0, chunks, one, 0)

            @pl.when(polar)
            def _():
                pack(0, k, order[SUBS:], SUBS)
                early_copy(0, k, 1).start()

            return carry

        lax.fori_loop(0, levels, mend_level, 0)

        def add_levels(index, carry):
            cols = pl.ds(pl.multiple_of(index * CHUNK, LANES), CHUNK)
            for group in range(groups):
                span = pl.ds(group * SUBS, SUBS)
                so_far = jnp.zeros((SUBS, CHUNK), jnp.float32)
                for k in reversed(range(levels)):
                    weight = (base_temp + new_fields[0, k, span, cols]) * thick[k]
                    geo[k, span, cols] = so_far + 0.5 * weight
                    so_far = so_far + weight
                below[span, cols] = so_far
            return carry

        lax.fori_loop(0, chunks, add_levels, 0)

        for by in range(1, lev_count):
            @pl.when(lev >= by)
            def _():
                col_copy(by).start()

        fill_slots(kept, half)

        def next_field(index, carry):
            q = 1 + index // levels
            k = levels - 1 - lax.rem(index, levels)
            cell_copy(q, k).wait()
            advect_level(q, k, True)

            @pl.when(polar & (q < last_q))
            def _():
                pack(q, k, order)
                for part in range(half // SUBS):
                    early_copy(q, k, part).start()

            return carry

        lax.fori_loop(0, slabs - levels, next_field, 0)

        def place_of(block):
            return lax.rem(block, per_segment) * LANES + PAD, block // per_segment

        def run(place):
            return pl.ds(pl.multiple_of(place * SUBS, SUBS), SUBS)

        def put_block(block, values):
            start, which = place_of(block)
            turned = values.T
            for v in range(LANES // SUBS):
                front[pl.ds((start + SUBS * v) * SUBS + which, SUBS, stride=SUBS), :] = turned[
                    SUBS * v : SUBS * (v + 1), :
                ]

        def get_block(block):
            start, which = place_of(block)
            return jnp.concatenate(
                [
                    front[pl.ds((start + SUBS * v) * SUBS + which, SUBS, stride=SUBS), :]
                    for v in range(LANES // SUBS)
                ],
                axis=0,
            ).T

        def cols_of(block):
            return pl.ds(pl.multiple_of(block * LANES, LANES), LANES)

        def one_pass(source, target, start, strength):
            def flux_of(west, slope, east):
                least = jnp.minimum(jnp.maximum(west, east), 0.0)
                most = jnp.maximum(jnp.minimum(west, east), 0.0)
                return strength * (slope - jnp.minimum(jnp.maximum(slope, least), most))

            def steps(index, state):
                cell, ahead, west, slope, inflow = state
                base = start + index * STEPS
                for j in range(STEPS):
                    beyond = source[run(base + j + 2), :]
                    east = beyond - ahead
                    outflow = flux_of(west, slope, east)
                    target[run(base + j), :] = cell + (outflow - inflow)
                    cell, ahead, west, slope, inflow = ahead, beyond, slope, east, outflow
                return cell, ahead, west, slope, inflow

            near = [source[run(start - 2 + j), :] for j in range(4)]
            slopes = [near[j + 1] - near[j] for j in range(3)]
            inflow = flux_of(slopes[0], slopes[1], slopes[2])
            lax.fori_loop(
                0, (length - SLACK) // STEPS, steps, (near[2], near[3], slopes[1], slopes[2], inflow)
            )

        def all_passes():
            for j in range(PAD):
                front[j * SUBS : (j + 1) * SUBS, :] = pltpu.roll(
                    front[(segment + j) * SUBS : (segment + j + 1) * SUBS, :], 1, 0
                )
                end = (PAD + segment + j) * SUBS
                front[end : end + SUBS, :] = pltpu.roll(
                    front[(PAD + j) * SUBS : (PAD + j + 1) * SUBS, :], SUBS - 1, 0
                )
            strength = factor[...]

            def pair(index, carry):
                one_pass(front, back, 2 + 4 * index, strength)
                one_pass(back, front, 4 + 4 * index, strength)
                return carry

            lax.fori_loop(0, PASSES // 2, pair, 0)

        @pl.when(plain)
        def _():
            factor_copy.wait_recv()

        def job(index, carry):
            q = lax.rem(index + last_q, nf)

            @pl.when(polar)
            def _():
                def fill(index, carry):
                    for block in (index * UNROLL + i for i in range(UNROLL)):
                        values = new_fields[q, :, :, cols_of(block)]
                        put_block(block, values.reshape(LANES, LANES))
                    return carry

                lax.fori_loop(0, blocks // UNROLL, fill, 0)

            @pl.when(plain & (index < last_q))
            def _():
                def heard(k, carry):
                    for part in range(half // SUBS):
                        early_copy(index, levels - 1 - k, part).wait_recv()
                    return carry

                lax.fori_loop(0, levels, heard, 0)

                def fill(place, carry):
                    for block in (place * UNROLL + i for i in range(UNROLL)):
                        values = landed[index, :, :, cols_of(block)].reshape(levels * half, LANES)
                        put_block(block, jnp.concatenate([values, values], axis=0))
                    return carry

                lax.fori_loop(0, blocks // UNROLL, fill, 0)

            @pl.when(polar | (index < last_q))
            def _():
                all_passes()

            @pl.when(polar)
            def _():
                def spill(place, carry):
                    for block in (place * UNROLL + i for i in range(UNROLL)):
                        new_fields[q, :, :, cols_of(block)] = get_block(block).reshape(
                            levels, rows, LANES
                        )
                    return carry

                lax.fori_loop(0, blocks // UNROLL, spill, 0)

                @pl.when(index == 0)
                def _():
                    def send(k, carry):
                        pack(last_q, k, range(half))
                        late_copy(k).start()
                        return carry

                    lax.fori_loop(0, levels, send, 0)

                def hold(k, carry):
                    keep(q, k)
                    return carry

                lax.fori_loop(0, levels, hold, 0)

            @pl.when(plain & (index < last_q))
            def _():
                def spill(place, carry):
                    for block in (place * UNROLL + i for i in range(UNROLL)):
                        values = get_block(block)
                        for k in range(levels):
                            one = values[k * half : (k + 1) * half, :]
                            whole = jnp.concatenate([one[half - 2 : half - 1], one[: half - 2], one[half - 1 :]], axis=0)
                            polar_rows[index, k, :, cols_of(block)] = whole
                    return carry

                lax.fori_loop(0, blocks // UNROLL, spill, 0)

            return carry

        lax.fori_loop(0, nf, job, 0)

        ground_copy.wait()
        for by in range(1, lev_count):
            @pl.when(lev + by < lev_count)
            def _():
                col_copy(by).wait_recv()

        def finish(index, carry):
            span = pl.ds(pl.multiple_of(index * SUBS, SUBS), SUBS)
            outside = ground[span, :]
            for by in range(1, lev_count):
                outside = outside + jnp.where(lev + by < lev_count, columns[by - 1, span, :], 0.0)
            for k in range(levels):
                geo[k, span, :] = geo[k, span, :] + outside
            return carry

        lax.fori_loop(0, groups, finish, 0)

        for by in range(1, lev_count):
            @pl.when(lev >= by)
            def _():
                col_copy(by).wait_send()

        @pl.when(jnp.logical_not(last))
        def _():
            north_copy.wait_send()

        @pl.when(jnp.logical_not(first))
        def _():
            south_copy.wait_send()

        @pl.when(polar)
        def _():
            factor_copy.wait_send()
            for q in range(last_q):
                for k in range(levels):
                    for part in range(half // SUBS):
                        early_copy(q, k, part).wait_send()
            for k in range(levels):
                late_copy(k).wait_send()

        @pl.when(plain)
        def _():
            for k in range(levels):
                late_copy(k).wait_recv()

    return kernel


def write_out(new_fields, geo, polar_rows, new_fields_out, geo_out, polar_rows_out, sem):
    levels = geo.shape[0]
    copies = []
    for k in range(levels):
        for q in range(new_fields.shape[0]):
            copies.append((new_fields.at[q, k], new_fields_out.at[q, k]))
            copies.append((polar_rows.at[q, k], polar_rows_out.at[q, k]))
        copies.append((geo.at[k], geo_out.at[k]))
    copies = [pltpu.make_async_copy(*pair, sem.at[i]) for i, pair in enumerate(copies)]
    for copy in copies:
        copy.start()
    for copy in copies:
        copy.wait()


def solution(mesh):
    lat_count, lev_count = mesh.shape["lat"], mesh.shape["lev"]

    def local(fields, velocity, surface, thickness, row_owner):
        nf, levels, rows, lons = fields.shape
        half = rows // 2
        length = lons // SUBS + 2 * PAD + SLACK
        hbm_spec = pl.BlockSpec(memory_space=pltpu.HBM)
        vmem_spec = pl.BlockSpec(memory_space=pltpu.VMEM)
        dma = pltpu.SemaphoreType.DMA
        f32 = jnp.float32
        shapes = ((nf, levels, rows, lons), (levels, rows, lons), (nf, levels, half, lons))
        held_bytes = sum(4 * math.prod(shape) for shape in shapes)
        held = pl.pallas_call(
            make_kernel(lat_count, lev_count, nf, levels, rows, lons),
            out_shape=tuple(pltpu.VMEM(shape, f32) for shape in shapes),
            in_specs=[hbm_spec] * 5,
            out_specs=[vmem_spec] * 3,
            scratch_shapes=[
                pltpu.VMEM((nf, levels, rows, lons), f32),
                pltpu.VMEM((2, levels, rows, lons), f32),
                pltpu.VMEM((rows, lons), f32),
                pltpu.VMEM((2, nf, levels, 1, lons), f32),
                pltpu.VMEM((rows, lons), f32),
                pltpu.VMEM((lev_count - 1, rows, lons), f32),
                pltpu.VMEM((nf, levels, half, lons), f32),
                pltpu.VMEM((nf - 1, levels, half, lons), f32),
                pltpu.VMEM((length * SUBS, LANES), f32),
                pltpu.VMEM((length * SUBS, LANES), f32),
                pltpu.VMEM((5, rows, LANES), f32),
                pltpu.VMEM((SUBS, LANES), f32),
                pltpu.VMEM((SUBS, LANES), f32),
                pltpu.SMEM((rows,), jnp.int32),
                pltpu.SMEM((levels,), f32),
                pltpu.SMEM((rows,), jnp.int32),
                dma((nf, levels)),
                dma((2, levels)),
                dma((3,)),
                dma((2,)),
                dma((2,)),
                dma((lev_count - 1,)),
                dma((lev_count - 1,)),
                dma((nf - 1, levels, half // SUBS)),
                dma((nf - 1, levels, half // SUBS)),
                dma((levels,)),
                dma((levels,)),
                dma((2,)),
            ],
            compiler_params=pltpu.CompilerParams(
                collective_id=0, has_side_effects=True, vmem_limit_bytes=67043328 - held_bytes
            ),
            name="step",
        )(fields, velocity, surface, thickness, row_owner)
        return pl.pallas_call(
            write_out,
            out_shape=tuple(jax.ShapeDtypeStruct(shape, f32) for shape in shapes),
            in_specs=[pl.BlockSpec(memory_space=pl.ANY)] * 3,
            out_specs=[hbm_spec] * 3,
            scratch_shapes=[dma((levels * (2 * nf + 1),))],
            compiler_params=pltpu.CompilerParams(vmem_limit_bytes=1024 * 1024),
            name="write",
        )(*held)

    in_specs = (
        P(None, "lev", "lat", None),
        P(None, "lev", "lat", None),
        P("lat", None),
        P("lev"),
        P("lat"),
    )
    out_specs = (P(None, "lev", "lat", None), P("lev", "lat", None), P(None, "lev", "lat", None))
    return jax.shard_map(local, mesh=mesh, in_specs=in_specs, out_specs=out_specs, check_vma=False)
```

```python
import math

import jax
import jax.numpy as jnp
from jax import lax
from jax.experimental import pallas as pl
from jax.experimental.pallas import tpu as pltpu
from jax.sharding import PartitionSpec as P

PASSES = 8
PAD = 2 * PASSES
SLACK = 32
STEPS = 68
LANES = 128
SUBS = 8
CHUNK = 512
UNROLL = 8
MESH = pl.DeviceIdType.MESH

courant_lon = 0.3
courant_lat = 0.3
diffuse_lon = 0.04
diffuse_lat = 0.08
base_temp = 3.0


def strength_of(row_ids, all_rows):
    cos_mid = jnp.cos(-0.5 * math.pi + (row_ids + 0.5) * (math.pi / all_rows))
    polar = (row_ids < all_rows // 4) | (row_ids >= all_rows - all_rows // 4)
    return jnp.where(polar, 0.05 + 0.2 * (1.0 - cos_mid / math.cos(0.25 * math.pi)), 0.0)


def make_kernel(lat_count, lev_count, nf, levels, rows, lons):
    half = rows // 2
    slabs = nf * levels
    groups = rows // SUBS
    all_rows = rows * lat_count
    spacing = math.pi / all_rows
    shift = lat_count // 2
    quarter = lat_count // 4
    blocks = lons // LANES
    per = CHUNK // LANES
    chunks = lons // CHUNK
    segment = lons // SUBS
    per_segment = segment // LANES
    length = segment + 2 * PAD + SLACK
    last_q = nf - 1
    order = list(range(1, half - 1)) + [0, half - 1]

    def kernel(
        fields, velocity, surface, thickness, row_owner,
        new_fields, geo, polar_rows,
        cells, wind, ground, halo, below, columns, packed, landed, front, back,
        tables, factor, factor_out, owners, thick, slots,
        detour, in_sem, halo_sem, col_sem, send_sem, recv_sem, factor_sem, detour_sem,
    ):
        me = lax.axis_index("lat")
        lev = lax.axis_index("lev")
        polar = (me < quarter) | (me >= lat_count - quarter)
        plain = jnp.logical_not(polar)
        partner = lax.rem(me + shift, lat_count)

        spans = (pl.ds(levels - 1, 1), pl.ds(levels - 2, 1), pl.ds(0, levels - 2))

        def load(index):
            span = spans[index]
            return (
                pltpu.make_async_copy(fields.at[0, span], cells.at[0, span], in_sem.at[2 * index]),
                pltpu.make_async_copy(velocity.at[:, span], wind.at[:, span], in_sem.at[2 * index + 1]),
            )

        others = pl.ds(1, nf - 1)
        load_others = pltpu.make_async_copy(fields.at[others], cells.at[others], in_sem.at[6])
        own_copy = pltpu.make_async_copy(row_owner, owners, in_sem.at[7])
        thick_copy = pltpu.make_async_copy(thickness, thick, in_sem.at[8])
        ground_copy = pltpu.make_async_copy(surface, ground, in_sem.at[9])

        barrier = pltpu.get_barrier_semaphore()
        for by in (shift, 1, lat_count - 1, quarter, lat_count - quarter):
            pl.semaphore_signal(
                barrier, inc=1, device_id={"lat": lax.rem(me + by, lat_count)}, device_id_type=MESH
            )
        for by in range(1, lev_count):
            pl.semaphore_signal(
                barrier, inc=1, device_id={"lev": lax.rem(lev + by, lev_count)}, device_id_type=MESH
            )

        own_copy.start()
        for index in range(3):
            for copy in load(index):
                copy.start()
        load_others.start()
        thick_copy.start()
        ground_copy.start()

        row_ids = (me * rows + lax.broadcasted_iota(jnp.int32, (rows, LANES), 0)).astype(jnp.float32)
        lat_mid = -0.5 * math.pi + (row_ids + 0.5) * spacing
        metric = 1.0 / jnp.maximum(jnp.cos(lat_mid), 0.25)
        to_north = diffuse_lat * metric * jnp.cos(lat_mid + 0.5 * spacing)
        to_south = diffuse_lat * metric * jnp.cos(lat_mid - 0.5 * spacing)
        to_side = diffuse_lon * metric * metric
        tables[0] = 0.5 * courant_lon * metric
        tables[1] = to_side
        tables[2] = to_north
        tables[3] = to_south
        tables[4] = 1.0 - 2.0 * to_side - to_north - to_south

        lane = lax.broadcasted_iota(jnp.int32, (SUBS, LANES), 1)
        for place in range(SLACK):
            at = (segment + 2 * PAD + place) * SUBS
            front[at : at + SUBS, :] = jnp.zeros((SUBS, LANES), jnp.float32)

        own_copy.wait()
        sent, kept = [], []
        for row in range(rows):
            away = (owners[row] != me).astype(jnp.int32)
            sent.append(away + (sent[-1] if row else 0))
            kept.append(row + 1 - sent[-1])

        def fill_slots(counts, base):
            for slot in range(half):
                place = jnp.int32(slot)
                for row in range(slot, slot + half):
                    place = place + (counts[row] <= slot).astype(jnp.int32)
                slots[base + slot] = place

        fill_slots(sent, 0)

        north_copy = pltpu.make_async_remote_copy(
            src_ref=fields.at[:, :, rows - 1 : rows, :], dst_ref=halo.at[0],
            send_sem=halo_sem.at[0], recv_sem=halo_sem.at[1],
            device_id={"lat": lax.rem(me + 1, lat_count)}, device_id_type=MESH,
        )
        south_copy = pltpu.make_async_remote_copy(
            src_ref=fields.at[:, :, 0:1, :], dst_ref=halo.at[1],
            send_sem=halo_sem.at[0], recv_sem=halo_sem.at[1],
            device_id={"lat": lax.rem(me + lat_count - 1, lat_count)}, device_id_type=MESH,
        )
        own_south = pltpu.make_async_copy(fields.at[:, :, 0:1, :], halo.at[0], halo_sem.at[1])
        own_north = pltpu.make_async_copy(fields.at[:, :, rows - 1 : rows, :], halo.at[1], halo_sem.at[1])
        first = me == 0
        last = me == lat_count - 1

        factor_copy = pltpu.make_async_remote_copy(
            src_ref=factor_out, dst_ref=factor, send_sem=factor_sem.at[0], recv_sem=factor_sem.at[1],
            device_id={"lat": partner}, device_id_type=MESH,
        )

        def row_copy(source, target, part, device=partner):
            return pltpu.make_async_remote_copy(
                src_ref=source, dst_ref=target, send_sem=send_sem.at[0], recv_sem=recv_sem.at[part],
                device_id={"lat": device}, device_id_type=MESH,
            )

        def early_copy(*place):
            return row_copy(packed.at[place], landed.at[place], place[0])

        def field_copy(q):
            return row_copy(packed.at[q], landed.at[q] if q < last_q else polar_rows.at[q], q)

        onward = lax.rem(me + quarter, lat_count)
        column = lax.rem(me, quarter) // 2
        turn = (last_q - 1, levels - 1, pl.ds(half - SUBS, SUBS))

        def detour_in(width):
            return pltpu.make_async_remote_copy(
                src_ref=packed.at[(*turn, pl.ds(0, width))], dst_ref=detour.at[:, pl.ds(0, width)],
                send_sem=send_sem.at[0], recv_sem=detour_sem.at[0],
                device_id={"lat": onward}, device_id_type=MESH,
            )

        def detour_out(width):
            return pltpu.make_async_remote_copy(
                src_ref=detour.at[:, pl.ds(0, width)], dst_ref=landed.at[(*turn, pl.ds(0, width))],
                send_sem=detour_sem.at[1], recv_sem=recv_sem.at[last_q - 1],
                device_id={"lat": onward}, device_id_type=MESH,
            )

        far = column == quarter // 2 - 1
        detours = ((lons // 2, (column > 0) & jnp.logical_not(far)), (3 * lons // 4, far))
        above = me >= lat_count - quarter
        under = me < quarter

        def col_copy(by):
            return pltpu.make_async_remote_copy(
                src_ref=below, dst_ref=columns.at[by - 1], send_sem=col_sem.at[0], recv_sem=col_sem.at[1],
                device_id={"lev": lax.rem(lev + lev_count - by, lev_count)}, device_id_type=MESH,
            )

        def col_copies(n):
            return pltpu.make_async_remote_copy(
                src_ref=columns.at[pl.ds(0, n)], dst_ref=columns.at[pl.ds(0, n)],
                send_sem=col_sem.at[0], recv_sem=col_sem.at[1],
                device_id={"lev": lax.rem(lev + 1, lev_count)}, device_id_type=MESH,
            )

        def halo_copies(ref):
            return pltpu.make_async_remote_copy(
                src_ref=ref, dst_ref=ref, send_sem=halo_sem.at[0], recv_sem=halo_sem.at[1],
                device_id={"lat": partner}, device_id_type=MESH,
            )

        sub = lax.broadcasted_iota(jnp.int32, (SUBS, CHUNK), 0)

        def advect_chunk(q, k, part, edges):
            cols = pl.ds(pl.multiple_of(part * CHUNK, LANES), CHUNK)
            left = pl.ds(pl.multiple_of(lax.rem(part * per + blocks - 1, blocks) * LANES, LANES), LANES)
            right = pl.ds(pl.multiple_of(lax.rem((part + 1) * per, blocks) * LANES, LANES), LANES)

            def spread(table, group):
                one = tables[table, group * SUBS : (group + 1) * SUBS, :]
                return jnp.concatenate([one] * per, axis=1)

            state = [cells[q, k, g * SUBS : (g + 1) * SUBS, cols] for g in range(groups)]
            up = [pltpu.roll(one, SUBS - 1, 0) for one in state]
            if edges:
                up.append(jnp.broadcast_to(halo[1, q, k, :, cols], (SUBS, CHUNK)))
                down = [jnp.broadcast_to(halo[0, q, k, :, cols], (SUBS, CHUNK))]
            else:
                up.append(state[groups - 1])
                down = [state[0]]
            down += [pltpu.roll(one, 1, 0) for one in state]
            for g in range(groups):
                span = pl.ds(g * SUBS, SUBS)
                wide = CHUNK + LANES
                east = pltpu.roll(jnp.concatenate([state[g], cells[q, k, span, right]], axis=1), wide - 1, 1)
                west = pltpu.roll(jnp.concatenate([cells[q, k, span, left], state[g]], axis=1), 1, 1)
                east, west = east[:, :CHUNK], west[:, LANES:]
                north = jnp.where(sub == SUBS - 1, up[g + 1], up[g])
                south = jnp.where(sub == 0, down[g], down[g + 1])
                along = spread(0, g) * wind[0, k, span, cols]
                across = (0.5 * courant_lat) * wind[1, k, span, cols]
                side = spread(1, g)
                result = (
                    spread(4, g) * state[g]
                    + ((side - along) * east + (side + along) * west)
                    + ((spread(2, g) - across) * north + (spread(3, g) + across) * south)
                )
                new_fields[q, k, span, cols] = result

        def advect_level(q, k, edges):
            def one(part, carry):
                advect_chunk(q, k, part, edges)
                return carry

            lax.fori_loop(0, chunks, one, 0)

        def pack(q, k, chosen, start=0, cols=slice(None)):
            for place, slot in enumerate(chosen):
                packed[q, k, start + place : start + place + 1, cols] = new_fields[
                    q, k, pl.ds(slots[slot], 1), cols
                ]

        def keep(q, k):
            for slot in range(half):
                polar_rows[q, k, slot : slot + 1, :] = new_fields[q, k, pl.ds(slots[half + slot], 1), :]

        def first_level(k):
            advect_level(0, k, False)

            @pl.when(polar)
            def _():
                pack(0, k, order[:SUBS])

        def send_first(k):
            @pl.when(polar)
            def _():
                early_copy(0, k, pl.ds(0, SUBS)).start()

        for copy in load(0):
            copy.wait()
        first_level(levels - 1)
        pl.semaphore_wait(barrier, 5 + lev_count - 1)
        send_first(levels - 1)

        @pl.when(jnp.logical_not(last))
        def _():
            north_copy.start()

        @pl.when(jnp.logical_not(first))
        def _():
            south_copy.start()

        @pl.when(first)
        def _():
            own_south.start()

        @pl.when(last)
        def _():
            own_north.start()

        def other_levels(index, carry):
            k = levels - 2 - index
            for stage in range(1, 3):
                @pl.when(index == stage - 1)
                def _():
                    for copy in load(stage):
                        copy.wait()

            first_level(k)
            send_first(k)
            return carry

        lax.fori_loop(0, levels - 1, other_levels, 0)

        @pl.when(polar)
        def _():
            here = lax.rem(lane, rows)
            away = jnp.zeros((SUBS, LANES), jnp.int32)
            slot_of = lax.rem(lane, half)
            for place, slot in enumerate(order):
                away = jnp.where(slot_of == place, slots[slot], away)
            factor[...] = strength_of((me * rows + here).astype(jnp.float32), all_rows)
            factor_out[...] = strength_of((me * rows + away).astype(jnp.float32), all_rows)

        @pl.when(polar)
        def _():
            factor_copy.start()

        halo_copies(halo).wait_recv()

        def mend_edges(k, part):
            cols = pl.ds(pl.multiple_of(part * CHUNK, LANES), CHUNK)
            for side, group, line, sign in ((0, 0, 0, 1.0), (1, groups - 1, SUBS - 1, -1.0)):
                span = pl.ds(group * SUBS, SUBS)
                table = tables[3 - side, span, :]
                weight = (
                    jnp.concatenate([table] * per, axis=1)
                    + (sign * 0.5 * courant_lat) * wind[1, k, span, cols]
                )
                beyond = jnp.broadcast_to(halo[side, 0, k, :, cols], (SUBS, CHUNK))
                change = weight * (beyond - cells[0, k, span, cols])
                new_fields[0, k, span, cols] = new_fields[0, k, span, cols] + jnp.where(
                    sub == line, change, 0.0
                )

        def mend_level(index, carry):
            k = levels - 1 - index

            def one(part, carry):
                mend_edges(k, part)
                return carry

            lax.fori_loop(0, chunks, one, 0)

            @pl.when(polar)
            def _():
                pack(0, k, order[SUBS:], SUBS)

            return carry

        lax.fori_loop(0, levels, mend_level, 0)

        @pl.when(polar)
        def _():
            early_copy(0, slice(None), pl.ds(SUBS, half - SUBS)).start()

        thick_copy.wait()

        def add_levels(index, carry):
            cols = pl.ds(pl.multiple_of(index * CHUNK, LANES), CHUNK)
            for group in range(groups):
                span = pl.ds(group * SUBS, SUBS)
                so_far = jnp.zeros((SUBS, CHUNK), jnp.float32)
                for k in reversed(range(levels)):
                    weight = (base_temp + new_fields[0, k, span, cols]) * thick[k]
                    geo[k, span, cols] = so_far + 0.5 * weight
                    so_far = so_far + weight
                below[span, cols] = so_far
            return carry

        lax.fori_loop(0, chunks, add_levels, 0)

        for by in range(1, lev_count):
            @pl.when(lev >= by)
            def _():
                col_copy(by).start()

        fill_slots(kept, half)

        load_others.wait()

        def next_field(index, carry):
            q = 1 + index // levels
            k = levels - 1 - lax.rem(index, levels)
            advect_level(q, k, True)

            @pl.when(polar & (q < last_q))
            def _():
                pack(q, k, order)

            return carry

        lax.fori_loop(0, levels, next_field, 0)

        for width, chosen in detours:
            @pl.when(above & chosen)
            def _():
                detour_in(width).start()
                early_copy(*turn, pl.ds(width, lons - width)).start()

        @pl.when(polar & jnp.logical_not(above & (column > 0)))
        def _():
            early_copy(*turn, slice(None)).start()

        @pl.when(polar)
        def _():
            early_copy(last_q - 1, levels - 1, pl.ds(0, half - SUBS)).start()
            early_copy(last_q - 1, pl.ds(0, levels - 1)).start()

        lax.fori_loop(levels, slabs - levels, next_field, 0)

        for width, chosen in detours:
            @pl.when(under & chosen)
            def _():
                detour_in(width).wait_recv()
                detour_out(width).start()

        def place_of(block):
            return lax.rem(block, per_segment) * LANES + PAD, block // per_segment

        def run(place):
            return pl.ds(pl.multiple_of(place * SUBS, SUBS), SUBS)

        def put_block(block, values):
            start, which = place_of(block)
            turned = values.T
            for v in range(LANES // SUBS):
                front[pl.ds((start + SUBS * v) * SUBS + which, SUBS, stride=SUBS), :] = turned[
                    SUBS * v : SUBS * (v + 1), :
                ]

        def get_block(block):
            start, which = place_of(block)
            return jnp.concatenate(
                [
                    front[pl.ds((start + SUBS * v) * SUBS + which, SUBS, stride=SUBS), :]
                    for v in range(LANES // SUBS)
                ],
                axis=0,
            ).T

        def cols_of(block):
            return pl.ds(pl.multiple_of(block * LANES, LANES), LANES)

        def one_pass(source, target, start, strength):
            def flux_of(west, slope, east):
                least = jnp.minimum(jnp.maximum(west, east), 0.0)
                most = jnp.maximum(jnp.minimum(west, east), 0.0)
                return strength * (slope - jnp.minimum(jnp.maximum(slope, least), most))

            def steps(index, state):
                cell, ahead, west, slope, inflow = state
                base = start + index * STEPS
                for j in range(STEPS):
                    beyond = source[run(base + j + 2), :]
                    east = beyond - ahead
                    outflow = flux_of(west, slope, east)
                    target[run(base + j), :] = cell + (outflow - inflow)
                    cell, ahead, west, slope, inflow = ahead, beyond, slope, east, outflow
                return cell, ahead, west, slope, inflow

            near = [source[run(start - 2 + j), :] for j in range(4)]
            slopes = [near[j + 1] - near[j] for j in range(3)]
            inflow = flux_of(slopes[0], slopes[1], slopes[2])
            lax.fori_loop(
                0, (length - SLACK) // STEPS, steps, (near[2], near[3], slopes[1], slopes[2], inflow)
            )

        def all_passes():
            for j in range(PAD):
                front[j * SUBS : (j + 1) * SUBS, :] = pltpu.roll(
                    front[(segment + j) * SUBS : (segment + j + 1) * SUBS, :], 1, 0
                )
                end = (PAD + segment + j) * SUBS
                front[end : end + SUBS, :] = pltpu.roll(
                    front[(PAD + j) * SUBS : (PAD + j + 1) * SUBS, :], SUBS - 1, 0
                )
            strength = factor[...]

            def pair(index, carry):
                one_pass(front, back, 2 + 4 * index, strength)
                one_pass(back, front, 4 + 4 * index, strength)
                return carry

            lax.fori_loop(0, PASSES // 2, pair, 0)

        @pl.when(plain)
        def _():
            factor_copy.wait_recv()

        def job(index, carry):
            q = lax.rem(index + last_q, nf)

            @pl.when(polar)
            def _():
                def fill(index, carry):
                    for block in (index * UNROLL + i for i in range(UNROLL)):
                        values = new_fields[q, :, :, cols_of(block)]
                        put_block(block, values.reshape(LANES, LANES))
                    return carry

                lax.fori_loop(0, blocks // UNROLL, fill, 0)

            @pl.when(plain & (index < last_q))
            def _():
                for q in range(last_q):
                    @pl.when(index == q)
                    def _():
                        field_copy(q).wait_recv()

                def fill(place, carry):
                    for block in (place * UNROLL + i for i in range(UNROLL)):
                        values = landed[index, :, :, cols_of(block)].reshape(levels * half, LANES)
                        put_block(block, jnp.concatenate([values, values], axis=0))
                    return carry

                lax.fori_loop(0, blocks // UNROLL, fill, 0)

            @pl.when(polar | (index < last_q))
            def _():
                all_passes()

            @pl.when(polar)
            def _():
                def spill(place, carry):
                    for block in (place * UNROLL + i for i in range(UNROLL)):
                        new_fields[q, :, :, cols_of(block)] = get_block(block).reshape(
                            levels, rows, LANES
                        )
                    return carry

                lax.fori_loop(0, blocks // UNROLL, spill, 0)

                @pl.when(index == 0)
                def _():
                    def send(k, carry):
                        pack(last_q, k, range(half))
                        return carry

                    lax.fori_loop(0, levels, send, 0)
                    field_copy(last_q).start()

                def hold(k, carry):
                    keep(q, k)
                    return carry

                lax.fori_loop(0, levels, hold, 0)

            @pl.when(plain & (index < last_q))
            def _():
                def spill(place, carry):
                    for block in (place * UNROLL + i for i in range(UNROLL)):
                        values = get_block(block)
                        for k in range(levels):
                            one = values[k * half : (k + 1) * half, :]
                            whole = jnp.concatenate([one[half - 2 : half - 1], one[: half - 2], one[half - 1 :]], axis=0)
                            polar_rows[index, k, :, cols_of(block)] = whole
                    return carry

                lax.fori_loop(0, blocks // UNROLL, spill, 0)

            return carry

        lax.fori_loop(0, nf, job, 0)

        ground_copy.wait()
        for n in range(1, lev_count):
            @pl.when(lev == lev_count - 1 - n)
            def _():
                col_copies(n).wait_recv()

        def finish(index, carry):
            span = pl.ds(pl.multiple_of(index * SUBS, SUBS), SUBS)
            outside = ground[span, :]
            for by in range(1, lev_count):
                outside = outside + jnp.where(lev + by < lev_count, columns[by - 1, span, :], 0.0)
            for k in range(levels):
                geo[k, span, :] = geo[k, span, :] + outside
            return carry

        lax.fori_loop(0, groups, finish, 0)

        for n in range(1, lev_count):
            @pl.when(lev == n)
            def _():
                col_copies(n).wait_send()

        @pl.when(first | last)
        def _():
            halo_copies(halo.at[0]).wait_send()

        @pl.when(jnp.logical_not(first | last))
        def _():
            halo_copies(halo).wait_send()

        for width, chosen in detours:
            @pl.when(under & chosen)
            def _():
                detour_out(width).wait_send()

        @pl.when(polar)
        def _():
            factor_copy.wait_send()
            row_copy(packed, polar_rows, last_q).wait_send()

        @pl.when(plain)
        def _():
            field_copy(last_q).wait_recv()

    return kernel


def write_out(new_fields, geo, polar_rows, new_fields_out, geo_out, polar_rows_out, sem):
    copies = [
        pltpu.make_async_copy(new_fields, new_fields_out, sem.at[0]),
        pltpu.make_async_copy(geo, geo_out, sem.at[1]),
        pltpu.make_async_copy(polar_rows, polar_rows_out, sem.at[2]),
    ]
    for copy in copies:
        copy.start()
    for copy in copies:
        copy.wait()


def solution(mesh):
    lat_count, lev_count = mesh.shape["lat"], mesh.shape["lev"]

    def local(fields, velocity, surface, thickness, row_owner):
        nf, levels, rows, lons = fields.shape
        half = rows // 2
        length = lons // SUBS + 2 * PAD + SLACK
        hbm_spec = pl.BlockSpec(memory_space=pltpu.HBM)
        vmem_spec = pl.BlockSpec(memory_space=pltpu.VMEM)
        dma = pltpu.SemaphoreType.DMA
        f32 = jnp.float32
        shapes = ((nf, levels, rows, lons), (levels, rows, lons), (nf, levels, half, lons))
        held_bytes = sum(4 * math.prod(shape) for shape in shapes)
        held = pl.pallas_call(
            make_kernel(lat_count, lev_count, nf, levels, rows, lons),
            out_shape=tuple(pltpu.VMEM(shape, f32) for shape in shapes),
            in_specs=[hbm_spec] * 5,
            out_specs=[vmem_spec] * 3,
            scratch_shapes=[
                pltpu.VMEM((nf, levels, rows, lons), f32),
                pltpu.VMEM((2, levels, rows, lons), f32),
                pltpu.VMEM((rows, lons), f32),
                pltpu.VMEM((2, nf, levels, 1, lons), f32),
                pltpu.VMEM((rows, lons), f32),
                pltpu.VMEM((lev_count - 1, rows, lons), f32),
                pltpu.VMEM((nf, levels, half, lons), f32),
                pltpu.VMEM((nf - 1, levels, half, lons), f32),
                pltpu.VMEM((length * SUBS, LANES), f32),
                pltpu.VMEM((length * SUBS, LANES), f32),
                pltpu.VMEM((5, rows, LANES), f32),
                pltpu.VMEM((SUBS, LANES), f32),
                pltpu.VMEM((SUBS, LANES), f32),
                pltpu.SMEM((rows,), jnp.int32),
                pltpu.SMEM((levels,), f32),
                pltpu.SMEM((rows,), jnp.int32),
                pltpu.VMEM((SUBS, 3 * lons // 4), f32),
                dma((10,)),
                dma((2,)),
                dma((2,)),
                dma((1,)),
                dma((nf,)),
                dma((2,)),
                dma((2,)),
            ],
            compiler_params=pltpu.CompilerParams(
                collective_id=0, has_side_effects=True, vmem_limit_bytes=67043328 - held_bytes
            ),
            name="step",
        )(fields, velocity, surface, thickness, row_owner)
        return pl.pallas_call(
            write_out,
            out_shape=tuple(jax.ShapeDtypeStruct(shape, f32) for shape in shapes),
            in_specs=[pl.BlockSpec(memory_space=pl.ANY)] * 3,
            out_specs=[hbm_spec] * 3,
            scratch_shapes=[dma((3,))],
            compiler_params=pltpu.CompilerParams(vmem_limit_bytes=1024 * 1024),
            name="write",
        )(*held)

    in_specs = (
        P(None, "lev", "lat", None),
        P(None, "lev", "lat", None),
        P("lat", None),
        P("lev"),
        P("lat"),
    )
    out_specs = (P(None, "lev", "lat", None), P("lev", "lat", None), P(None, "lev", "lat", None))
    return jax.shard_map(local, mesh=mesh, in_specs=in_specs, out_specs=out_specs, check_vma=False)
```

```python
import math

import jax
import jax.numpy as jnp
from jax import lax
from jax.experimental import pallas as pl
from jax.experimental.pallas import tpu as pltpu
from jax.sharding import PartitionSpec as P

PASSES = 8
PAD = 2 * PASSES
SLACK = 32
STEPS = 68
LANES = 128
SUBS = 8
CHUNK = 512
UNROLL = 8
MESH = pl.DeviceIdType.MESH

courant_lon = 0.3
courant_lat = 0.3
diffuse_lon = 0.04
diffuse_lat = 0.08
base_temp = 3.0


def strength_of(row_ids, all_rows):
    cos_mid = jnp.cos(-0.5 * math.pi + (row_ids + 0.5) * (math.pi / all_rows))
    polar = (row_ids < all_rows // 4) | (row_ids >= all_rows - all_rows // 4)
    return jnp.where(polar, 0.05 + 0.2 * (1.0 - cos_mid / math.cos(0.25 * math.pi)), 0.0)


def make_kernel(lat_count, lev_count, nf, levels, rows, lons):
    half = rows // 2
    slabs = nf * levels
    groups = rows // SUBS
    all_rows = rows * lat_count
    spacing = math.pi / all_rows
    shift = lat_count // 2
    quarter = lat_count // 4
    blocks = lons // LANES
    per = CHUNK // LANES
    chunks = lons // CHUNK
    segment = lons // SUBS
    per_segment = segment // LANES
    length = segment + 2 * PAD + SLACK
    last_q = nf - 1
    order = list(range(1, half - 1)) + [0, half - 1]

    def kernel(
        fields, velocity, surface, thickness, row_owner,
        new_fields, geo, polar_rows,
        cells, wind, ground, halo, below, columns, packed, landed, front, back,
        tables, factor, factor_out, owners, thick, slots,
        detour, passing, pass_sem, in_sem, halo_sem, col_sem, send_sem, recv_sem, factor_sem, detour_sem,
    ):
        me = lax.axis_index("lat")
        lev = lax.axis_index("lev")
        polar = (me < quarter) | (me >= lat_count - quarter)
        plain = jnp.logical_not(polar)
        partner = lax.rem(me + shift, lat_count)

        spans = (pl.ds(levels - 1, 1), pl.ds(levels - 2, 1), pl.ds(0, levels - 2))

        def load(index):
            span = spans[index]
            return (
                pltpu.make_async_copy(fields.at[0, span], cells.at[0, span], in_sem.at[2 * index]),
                pltpu.make_async_copy(velocity.at[:, span], wind.at[:, span], in_sem.at[2 * index + 1]),
            )

        others = pl.ds(1, nf - 1)
        load_others = pltpu.make_async_copy(fields.at[others], cells.at[others], in_sem.at[6])
        own_copy = pltpu.make_async_copy(row_owner, owners, in_sem.at[7])
        thick_copy = pltpu.make_async_copy(thickness, thick, in_sem.at[8])
        ground_copy = pltpu.make_async_copy(surface, ground, in_sem.at[9])

        barrier = pltpu.get_barrier_semaphore()
        first = me == 0
        last = me == lat_count - 1
        for by in (shift, quarter, lat_count - quarter):
            pl.semaphore_signal(
                barrier, inc=1, device_id={"lat": lax.rem(me + by, lat_count)}, device_id_type=MESH
            )

        @pl.when(jnp.logical_not(last))
        def _():
            pl.semaphore_signal(barrier, inc=1, device_id={"lat": me + 1}, device_id_type=MESH)

        @pl.when(jnp.logical_not(first))
        def _():
            pl.semaphore_signal(barrier, inc=1, device_id={"lat": me - 1}, device_id_type=MESH)

        middle = 2 * quarter
        routes = (
            (0, quarter - 1, quarter + 4, levels // 2),
            (1, lat_count - quarter, middle + 2, levels // 2),
            (0, middle - 1, middle + 4, levels // 2),
            (1, middle, quarter + 2, levels // 2),
        )
        greetings = {}
        for side, sender, via, _ in routes:
            target = sender + (1, -1)[side]
            for one, other in ((sender, via), (via, target)):
                greetings.setdefault(one, []).append(other)
                greetings.setdefault(other, []).append(one)
        for here, friends in greetings.items():
            @pl.when(me == here)
            def _():
                for there in friends:
                    pl.semaphore_signal(
                        barrier, inc=1, device_id={"lat": there}, device_id_type=MESH
                    )

        for by in range(1, lev_count):
            pl.semaphore_signal(
                barrier, inc=1, device_id={"lev": lax.rem(lev + by, lev_count)}, device_id_type=MESH
            )

        own_copy.start()
        for index in range(3):
            for copy in load(index):
                copy.start()
        load_others.start()
        thick_copy.start()
        ground_copy.start()

        row_ids = (me * rows + lax.broadcasted_iota(jnp.int32, (rows, LANES), 0)).astype(jnp.float32)
        lat_mid = -0.5 * math.pi + (row_ids + 0.5) * spacing
        metric = 1.0 / jnp.maximum(jnp.cos(lat_mid), 0.25)
        to_north = diffuse_lat * metric * jnp.cos(lat_mid + 0.5 * spacing)
        to_south = diffuse_lat * metric * jnp.cos(lat_mid - 0.5 * spacing)
        to_side = diffuse_lon * metric * metric
        tables[0] = 0.5 * courant_lon * metric
        tables[1] = to_side
        tables[2] = to_north
        tables[3] = to_south
        tables[4] = 1.0 - 2.0 * to_side - to_north - to_south

        lane = lax.broadcasted_iota(jnp.int32, (SUBS, LANES), 1)
        for place in range(SLACK):
            at = (segment + 2 * PAD + place) * SUBS
            front[at : at + SUBS, :] = jnp.zeros((SUBS, LANES), jnp.float32)

        own_copy.wait()
        sent, kept = [], []
        for row in range(rows):
            away = (owners[row] != me).astype(jnp.int32)
            sent.append(away + (sent[-1] if row else 0))
            kept.append(row + 1 - sent[-1])

        def fill_slots(counts, base):
            for slot in range(half):
                place = jnp.int32(slot)
                for row in range(slot, slot + half):
                    place = place + (counts[row] <= slot).astype(jnp.int32)
                slots[base + slot] = place

        fill_slots(sent, 0)

        every = pl.ds(0, levels)
        edge = (pl.ds(rows - 1, 1), pl.ds(0, 1))

        def halo_copy(side, span):
            return pltpu.make_async_remote_copy(
                src_ref=fields.at[:, span, edge[side], :], dst_ref=halo.at[side, :, span],
                send_sem=halo_sem.at[0], recv_sem=halo_sem.at[1],
                device_id={"lat": lax.rem(me + (1, lat_count - 1)[side], lat_count)}, device_id_type=MESH,
            )

        def pass_in(side, sender, via, count):
            return pltpu.make_async_remote_copy(
                src_ref=fields.at[:, pl.ds(0, count), edge[side], :], dst_ref=passing.at[:, pl.ds(0, count)],
                send_sem=halo_sem.at[0], recv_sem=pass_sem.at[0],
                device_id={"lat": via}, device_id_type=MESH,
            )

        def pass_out(side, sender, via, count):
            return pltpu.make_async_remote_copy(
                src_ref=passing.at[:, pl.ds(0, count)], dst_ref=halo.at[side, :, pl.ds(0, count)],
                send_sem=pass_sem.at[1], recv_sem=halo_sem.at[1],
                device_id={"lat": sender + (1, -1)[side]}, device_id_type=MESH,
            )

        own_south = pltpu.make_async_copy(fields.at[:, :, 0:1, :], halo.at[0], halo_sem.at[1])
        own_north = pltpu.make_async_copy(fields.at[:, :, rows - 1 : rows, :], halo.at[1], halo_sem.at[1])

        factor_copy = pltpu.make_async_remote_copy(
            src_ref=factor_out, dst_ref=factor, send_sem=factor_sem.at[0], recv_sem=factor_sem.at[1],
            device_id={"lat": partner}, device_id_type=MESH,
        )

        def row_copy(source, target, part, device=partner):
            return pltpu.make_async_remote_copy(
                src_ref=source, dst_ref=target, send_sem=send_sem.at[0], recv_sem=recv_sem.at[part],
                device_id={"lat": device}, device_id_type=MESH,
            )

        def early_copy(*place):
            return row_copy(packed.at[place], landed.at[place], place[0])

        def field_copy(q):
            return row_copy(packed.at[q], landed.at[q] if q < last_q else polar_rows.at[q], q)

        onward = lax.rem(me + quarter, lat_count)
        column = lax.rem(me, quarter) // 2
        turn = (last_q - 1, levels - 1, pl.ds(half - SUBS, SUBS))

        def detour_in(width):
            return pltpu.make_async_remote_copy(
                src_ref=packed.at[(*turn, pl.ds(0, width))], dst_ref=detour.at[:, pl.ds(0, width)],
                send_sem=send_sem.at[0], recv_sem=detour_sem.at[0],
                device_id={"lat": onward}, device_id_type=MESH,
            )

        def detour_out(width):
            return pltpu.make_async_remote_copy(
                src_ref=detour.at[:, pl.ds(0, width)], dst_ref=landed.at[(*turn, pl.ds(0, width))],
                send_sem=detour_sem.at[1], recv_sem=recv_sem.at[last_q - 1],
                device_id={"lat": onward}, device_id_type=MESH,
            )

        odd = lax.rem(column, 2) == 1
        detours = ((lons // 4, jnp.logical_not(odd)), (5 * lons // 8, odd))
        above = me >= lat_count - quarter
        under = me < quarter

        def col_copy(by):
            return pltpu.make_async_remote_copy(
                src_ref=below, dst_ref=columns.at[by - 1], send_sem=col_sem.at[0], recv_sem=col_sem.at[1],
                device_id={"lev": lax.rem(lev + lev_count - by, lev_count)}, device_id_type=MESH,
            )

        def col_copies(n):
            return pltpu.make_async_remote_copy(
                src_ref=columns.at[pl.ds(0, n)], dst_ref=columns.at[pl.ds(0, n)],
                send_sem=col_sem.at[0], recv_sem=col_sem.at[1],
                device_id={"lev": lax.rem(lev + 1, lev_count)}, device_id_type=MESH,
            )

        def halo_copies(ref):
            return pltpu.make_async_remote_copy(
                src_ref=ref, dst_ref=ref, send_sem=halo_sem.at[0], recv_sem=halo_sem.at[1],
                device_id={"lat": partner}, device_id_type=MESH,
            )

        sub = lax.broadcasted_iota(jnp.int32, (SUBS, CHUNK), 0)

        def advect_chunk(q, k, part, edges):
            cols = pl.ds(pl.multiple_of(part * CHUNK, LANES), CHUNK)
            left = pl.ds(pl.multiple_of(lax.rem(part * per + blocks - 1, blocks) * LANES, LANES), LANES)
            right = pl.ds(pl.multiple_of(lax.rem((part + 1) * per, blocks) * LANES, LANES), LANES)

            def spread(table, group):
                one = tables[table, group * SUBS : (group + 1) * SUBS, :]
                return jnp.concatenate([one] * per, axis=1)

            state = [cells[q, k, g * SUBS : (g + 1) * SUBS, cols] for g in range(groups)]
            up = [pltpu.roll(one, SUBS - 1, 0) for one in state]
            if edges:
                up.append(jnp.broadcast_to(halo[1, q, k, :, cols], (SUBS, CHUNK)))
                down = [jnp.broadcast_to(halo[0, q, k, :, cols], (SUBS, CHUNK))]
            else:
                up.append(state[groups - 1])
                down = [state[0]]
            down += [pltpu.roll(one, 1, 0) for one in state]
            for g in range(groups):
                span = pl.ds(g * SUBS, SUBS)
                wide = CHUNK + LANES
                east = pltpu.roll(jnp.concatenate([state[g], cells[q, k, span, right]], axis=1), wide - 1, 1)
                west = pltpu.roll(jnp.concatenate([cells[q, k, span, left], state[g]], axis=1), 1, 1)
                east, west = east[:, :CHUNK], west[:, LANES:]
                north = jnp.where(sub == SUBS - 1, up[g + 1], up[g])
                south = jnp.where(sub == 0, down[g], down[g + 1])
                along = spread(0, g) * wind[0, k, span, cols]
                across = (0.5 * courant_lat) * wind[1, k, span, cols]
                side = spread(1, g)
                result = (
                    spread(4, g) * state[g]
                    + ((side - along) * east + (side + along) * west)
                    + ((spread(2, g) - across) * north + (spread(3, g) + across) * south)
                )
                new_fields[q, k, span, cols] = result

        def advect_level(q, k, edges):
            def one(part, carry):
                advect_chunk(q, k, part, edges)
                return carry

            lax.fori_loop(0, chunks, one, 0)

        def pack(q, k, chosen, start=0, cols=slice(None)):
            for place, slot in enumerate(chosen):
                packed[q, k, start + place : start + place + 1, cols] = new_fields[
                    q, k, pl.ds(slots[slot], 1), cols
                ]

        def keep(q, k):
            for slot in range(half):
                polar_rows[q, k, slot : slot + 1, :] = new_fields[q, k, pl.ds(slots[half + slot], 1), :]

        def first_level(k):
            advect_level(0, k, False)

            @pl.when(polar)
            def _():
                pack(0, k, order[:SUBS])

        def send_first(k):
            @pl.when(polar)
            def _():
                early_copy(0, k, pl.ds(0, SUBS)).start()

        for copy in load(0):
            copy.wait()
        first_level(levels - 1)

        heard = 5 + lev_count - 1 - (first | last).astype(jnp.int32)
        for here, friends in greetings.items():
            heard = heard + (me == here).astype(jnp.int32) * len(friends)
        pl.semaphore_wait(barrier, heard)
        send_first(levels - 1)

        for side, end in ((0, last), (1, first)):
            whole = jnp.logical_not(end)
            for route in routes:
                if route[0] == side:
                    whole = whole & (me != route[1])

            @pl.when(whole)
            def _():
                halo_copy(side, every).start()

        for route in routes:
            @pl.when(me == route[1])
            def _():
                pass_in(*route).start()
                halo_copy(route[0], pl.ds(route[3], levels - route[3])).start()

        @pl.when(first)
        def _():
            own_south.start()

        @pl.when(last)
        def _():
            own_north.start()

        def other_levels(index, carry):
            k = levels - 2 - index
            for stage in range(1, 3):
                @pl.when(index == stage - 1)
                def _():
                    for copy in load(stage):
                        copy.wait()

            first_level(k)
            send_first(k)
            return carry

        lax.fori_loop(0, levels - 1, other_levels, 0)

        @pl.when(polar)
        def _():
            here = lax.rem(lane, rows)
            away = jnp.zeros((SUBS, LANES), jnp.int32)
            slot_of = lax.rem(lane, half)
            for place, slot in enumerate(order):
                away = jnp.where(slot_of == place, slots[slot], away)
            factor[...] = strength_of((me * rows + here).astype(jnp.float32), all_rows)
            factor_out[...] = strength_of((me * rows + away).astype(jnp.float32), all_rows)

        @pl.when(polar)
        def _():
            factor_copy.start()

        for route in routes:
            @pl.when(me == route[2])
            def _():
                pass_in(*route).wait_recv()
                pass_out(*route).start()

        halo_copies(halo).wait_recv()

        def mend_edges(k, part):
            cols = pl.ds(pl.multiple_of(part * CHUNK, LANES), CHUNK)
            for side, group, line, sign in ((0, 0, 0, 1.0), (1, groups - 1, SUBS - 1, -1.0)):
                span = pl.ds(group * SUBS, SUBS)
                table = tables[3 - side, span, :]
                weight = (
                    jnp.concatenate([table] * per, axis=1)
                    + (sign * 0.5 * courant_lat) * wind[1, k, span, cols]
                )
                beyond = jnp.broadcast_to(halo[side, 0, k, :, cols], (SUBS, CHUNK))
                change = weight * (beyond - cells[0, k, span, cols])
                new_fields[0, k, span, cols] = new_fields[0, k, span, cols] + jnp.where(
                    sub == line, change, 0.0
                )

        def mend_level(index, carry):
            k = levels - 1 - index

            def one(part, carry):
                mend_edges(k, part)
                return carry

            lax.fori_loop(0, chunks, one, 0)

            @pl.when(polar)
            def _():
                pack(0, k, order[SUBS:], SUBS)

            return carry

        lax.fori_loop(0, levels, mend_level, 0)

        @pl.when(polar)
        def _():
            early_copy(0, slice(None), pl.ds(SUBS, half - SUBS)).start()

        thick_copy.wait()

        def add_levels(index, carry):
            cols = pl.ds(pl.multiple_of(index * CHUNK, LANES), CHUNK)
            for group in range(groups):
                span = pl.ds(group * SUBS, SUBS)
                so_far = jnp.zeros((SUBS, CHUNK), jnp.float32)
                for k in reversed(range(levels)):
                    weight = (base_temp + new_fields[0, k, span, cols]) * thick[k]
                    geo[k, span, cols] = so_far + 0.5 * weight
                    so_far = so_far + weight
                below[span, cols] = so_far
            return carry

        lax.fori_loop(0, chunks, add_levels, 0)

        for by in range(1, lev_count):
            @pl.when(lev >= by)
            def _():
                col_copy(by).start()

        fill_slots(kept, half)

        load_others.wait()

        def next_field(index, carry):
            q = 1 + index // levels
            k = levels - 1 - lax.rem(index, levels)
            advect_level(q, k, True)

            @pl.when(polar & (q < last_q))
            def _():
                pack(q, k, order)

            return carry

        lax.fori_loop(0, levels, next_field, 0)

        for width, chosen in detours:
            @pl.when(above & chosen)
            def _():
                detour_in(width).start()
                early_copy(*turn, pl.ds(width, lons - width)).start()

        @pl.when(polar & jnp.logical_not(above))
        def _():
            early_copy(*turn, slice(None)).start()

        @pl.when(polar)
        def _():
            early_copy(last_q - 1, levels - 1, pl.ds(0, half - SUBS)).start()
            early_copy(last_q - 1, pl.ds(0, levels - 1)).start()

        lax.fori_loop(levels, slabs - levels, next_field, 0)

        for width, chosen in detours:
            @pl.when(under & chosen)
            def _():
                detour_in(width).wait_recv()
                detour_out(width).start()

        def place_of(block):
            return lax.rem(block, per_segment) * LANES + PAD, block // per_segment

        def run(place):
            return pl.ds(pl.multiple_of(place * SUBS, SUBS), SUBS)

        def put_block(block, values):
            start, which = place_of(block)
            turned = values.T
            for v in range(LANES // SUBS):
                front[pl.ds((start + SUBS * v) * SUBS + which, SUBS, stride=SUBS), :] = turned[
                    SUBS * v : SUBS * (v + 1), :
                ]

        def get_block(block):
            start, which = place_of(block)
            return jnp.concatenate(
                [
                    front[pl.ds((start + SUBS * v) * SUBS + which, SUBS, stride=SUBS), :]
                    for v in range(LANES // SUBS)
                ],
                axis=0,
            ).T

        def cols_of(block):
            return pl.ds(pl.multiple_of(block * LANES, LANES), LANES)

        def one_pass(source, target, start, strength):
            def flux_of(west, slope, east):
                least = jnp.minimum(jnp.maximum(west, east), 0.0)
                most = jnp.maximum(jnp.minimum(west, east), 0.0)
                return strength * (slope - jnp.minimum(jnp.maximum(slope, least), most))

            def steps(index, state):
                cell, ahead, west, slope, inflow = state
                base = start + index * STEPS
                for j in range(STEPS):
                    beyond = source[run(base + j + 2), :]
                    east = beyond - ahead
                    outflow = flux_of(west, slope, east)
                    target[run(base + j), :] = cell + (outflow - inflow)
                    cell, ahead, west, slope, inflow = ahead, beyond, slope, east, outflow
                return cell, ahead, west, slope, inflow

            near = [source[run(start - 2 + j), :] for j in range(4)]
            slopes = [near[j + 1] - near[j] for j in range(3)]
            inflow = flux_of(slopes[0], slopes[1], slopes[2])
            lax.fori_loop(
                0, (length - SLACK) // STEPS, steps, (near[2], near[3], slopes[1], slopes[2], inflow)
            )

        def all_passes():
            for j in range(PAD):
                front[j * SUBS : (j + 1) * SUBS, :] = pltpu.roll(
                    front[(segment + j) * SUBS : (segment + j + 1) * SUBS, :], 1, 0
                )
                end = (PAD + segment + j) * SUBS
                front[end : end + SUBS, :] = pltpu.roll(
                    front[(PAD + j) * SUBS : (PAD + j + 1) * SUBS, :], SUBS - 1, 0
                )
            strength = factor[...]

            def pair(index, carry):
                one_pass(front, back, 2 + 4 * index, strength)
                one_pass(back, front, 4 + 4 * index, strength)
                return carry

            lax.fori_loop(0, PASSES // 2, pair, 0)

        @pl.when(plain)
        def _():
            factor_copy.wait_recv()

        def job(index, carry):
            q = lax.rem(index + last_q, nf)

            @pl.when(polar)
            def _():
                def fill(index, carry):
                    for block in (index * UNROLL + i for i in range(UNROLL)):
                        values = new_fields[q, :, :, cols_of(block)]
                        put_block(block, values.reshape(LANES, LANES))
                    return carry

                lax.fori_loop(0, blocks // UNROLL, fill, 0)

            @pl.when(plain & (index < last_q))
            def _():
                for q in range(last_q):
                    @pl.when(index == q)
                    def _():
                        field_copy(q).wait_recv()

                def fill(place, carry):
                    for block in (place * UNROLL + i for i in range(UNROLL)):
                        values = landed[index, :, :, cols_of(block)].reshape(levels * half, LANES)
                        put_block(block, jnp.concatenate([values, values], axis=0))
                    return carry

                lax.fori_loop(0, blocks // UNROLL, fill, 0)

            @pl.when(polar | (index < last_q))
            def _():
                all_passes()

            @pl.when(polar)
            def _():
                def spill(place, carry):
                    for block in (place * UNROLL + i for i in range(UNROLL)):
                        new_fields[q, :, :, cols_of(block)] = get_block(block).reshape(
                            levels, rows, LANES
                        )
                    return carry

                lax.fori_loop(0, blocks // UNROLL, spill, 0)

                @pl.when(index == 0)
                def _():
                    def send(k, carry):
                        pack(last_q, k, range(half))
                        return carry

                    lax.fori_loop(0, levels, send, 0)
                    field_copy(last_q).start()

                def hold(k, carry):
                    keep(q, k)
                    return carry

                lax.fori_loop(0, levels, hold, 0)

            @pl.when(plain & (index < last_q))
            def _():
                def spill(place, carry):
                    for block in (place * UNROLL + i for i in range(UNROLL)):
                        values = get_block(block)
                        for k in range(levels):
                            one = values[k * half : (k + 1) * half, :]
                            whole = jnp.concatenate([one[half - 2 : half - 1], one[: half - 2], one[half - 1 :]], axis=0)
                            polar_rows[index, k, :, cols_of(block)] = whole
                    return carry

                lax.fori_loop(0, blocks // UNROLL, spill, 0)

            return carry

        lax.fori_loop(0, nf, job, 0)

        ground_copy.wait()
        for n in range(1, lev_count):
            @pl.when(lev == lev_count - 1 - n)
            def _():
                col_copies(n).wait_recv()

        def finish(index, carry):
            span = pl.ds(pl.multiple_of(index * SUBS, SUBS), SUBS)
            outside = ground[span, :]
            for by in range(1, lev_count):
                outside = outside + jnp.where(lev + by < lev_count, columns[by - 1, span, :], 0.0)
            for k in range(levels):
                geo[k, span, :] = geo[k, span, :] + outside
            return carry

        lax.fori_loop(0, groups, finish, 0)

        for n in range(1, lev_count):
            @pl.when(lev == n)
            def _():
                col_copies(n).wait_send()

        @pl.when(first | last)
        def _():
            halo_copies(halo.at[0]).wait_send()

        @pl.when(jnp.logical_not(first | last))
        def _():
            halo_copies(halo).wait_send()

        for route in routes:
            @pl.when(me == route[2])
            def _():
                pass_out(*route).wait_send()

        for width, chosen in detours:
            @pl.when(under & chosen)
            def _():
                detour_out(width).wait_send()

        @pl.when(polar)
        def _():
            factor_copy.wait_send()
            row_copy(packed, polar_rows, last_q).wait_send()

        @pl.when(plain)
        def _():
            field_copy(last_q).wait_recv()

    return kernel


def write_out(new_fields, geo, polar_rows, new_fields_out, geo_out, polar_rows_out, sem):
    copies = [
        pltpu.make_async_copy(new_fields, new_fields_out, sem.at[0]),
        pltpu.make_async_copy(geo, geo_out, sem.at[1]),
        pltpu.make_async_copy(polar_rows, polar_rows_out, sem.at[2]),
    ]
    for copy in copies:
        copy.start()
    for copy in copies:
        copy.wait()


def solution(mesh):
    lat_count, lev_count = mesh.shape["lat"], mesh.shape["lev"]

    def local(fields, velocity, surface, thickness, row_owner):
        nf, levels, rows, lons = fields.shape
        half = rows // 2
        length = lons // SUBS + 2 * PAD + SLACK
        hbm_spec = pl.BlockSpec(memory_space=pltpu.HBM)
        vmem_spec = pl.BlockSpec(memory_space=pltpu.VMEM)
        dma = pltpu.SemaphoreType.DMA
        f32 = jnp.float32
        shapes = ((nf, levels, rows, lons), (levels, rows, lons), (nf, levels, half, lons))
        held_bytes = sum(4 * math.prod(shape) for shape in shapes)
        held = pl.pallas_call(
            make_kernel(lat_count, lev_count, nf, levels, rows, lons),
            out_shape=tuple(pltpu.VMEM(shape, f32) for shape in shapes),
            in_specs=[hbm_spec] * 5,
            out_specs=[vmem_spec] * 3,
            scratch_shapes=[
                pltpu.VMEM((nf, levels, rows, lons), f32),
                pltpu.VMEM((2, levels, rows, lons), f32),
                pltpu.VMEM((rows, lons), f32),
                pltpu.VMEM((2, nf, levels, 1, lons), f32),
                pltpu.VMEM((rows, lons), f32),
                pltpu.VMEM((lev_count - 1, rows, lons), f32),
                pltpu.VMEM((nf, levels, half, lons), f32),
                pltpu.VMEM((nf - 1, levels, half, lons), f32),
                pltpu.VMEM((length * SUBS, LANES), f32),
                pltpu.VMEM((length * SUBS, LANES), f32),
                pltpu.VMEM((5, rows, LANES), f32),
                pltpu.VMEM((SUBS, LANES), f32),
                pltpu.VMEM((SUBS, LANES), f32),
                pltpu.SMEM((rows,), jnp.int32),
                pltpu.SMEM((levels,), f32),
                pltpu.SMEM((rows,), jnp.int32),
                pltpu.VMEM((SUBS, 5 * lons // 8), f32),
                pltpu.VMEM((nf, levels // 2, 1, lons), f32),
                dma((2,)),
                dma((10,)),
                dma((2,)),
                dma((2,)),
                dma((1,)),
                dma((nf,)),
                dma((2,)),
                dma((2,)),
            ],
            compiler_params=pltpu.CompilerParams(
                collective_id=0, has_side_effects=True, vmem_limit_bytes=67043328 - held_bytes
            ),
            name="step",
        )(fields, velocity, surface, thickness, row_owner)
        return pl.pallas_call(
            write_out,
            out_shape=tuple(jax.ShapeDtypeStruct(shape, f32) for shape in shapes),
            in_specs=[pl.BlockSpec(memory_space=pl.ANY)] * 3,
            out_specs=[hbm_spec] * 3,
            scratch_shapes=[dma((3,))],
            compiler_params=pltpu.CompilerParams(vmem_limit_bytes=1024 * 1024),
            name="write",
        )(*held)

    in_specs = (
        P(None, "lev", "lat", None),
        P(None, "lev", "lat", None),
        P("lat", None),
        P("lev"),
        P("lat"),
    )
    out_specs = (P(None, "lev", "lat", None), P("lev", "lat", None), P(None, "lev", "lat", None))
    return jax.shard_map(local, mesh=mesh, in_specs=in_specs, out_specs=out_specs, check_vma=False)
```

```python
import math

import jax
import jax.numpy as jnp
from jax import lax
from jax.experimental import pallas as pl
from jax.experimental.pallas import tpu as pltpu
from jax.sharding import PartitionSpec as P

PASSES = 8
PAD = 2 * PASSES
SLACK = 32
STEPS = 68
LANES = 128
SUBS = 8
CHUNK = 512
UNROLL = 8
MESH = pl.DeviceIdType.MESH

courant_lon = 0.3
courant_lat = 0.3
diffuse_lon = 0.04
diffuse_lat = 0.08
base_temp = 3.0


def strength_of(row_ids, all_rows):
    cos_mid = jnp.cos(-0.5 * math.pi + (row_ids + 0.5) * (math.pi / all_rows))
    polar = (row_ids < all_rows // 4) | (row_ids >= all_rows - all_rows // 4)
    return jnp.where(polar, 0.05 + 0.2 * (1.0 - cos_mid / math.cos(0.25 * math.pi)), 0.0)


def make_kernel(lat_count, lev_count, nf, levels, rows, lons):
    half = rows // 2
    slabs = nf * levels
    groups = rows // SUBS
    all_rows = rows * lat_count
    spacing = math.pi / all_rows
    shift = lat_count // 2
    quarter = lat_count // 4
    blocks = lons // LANES
    per = CHUNK // LANES
    chunks = lons // CHUNK
    segment = lons // SUBS
    per_segment = segment // LANES
    length = segment + 2 * PAD + SLACK
    last_q = nf - 1
    order = list(range(1, half - 1)) + [0, half - 1]

    def kernel(
        fields, velocity, surface, thickness, row_owner,
        new_fields, geo, polar_rows,
        cells, wind, ground, halo, below, columns, packed, landed, front, back,
        tables, factor, factor_out, owners, thick, slots,
        detour, passing, pass_sem, in_sem, halo_sem, col_sem, send_sem, recv_sem, factor_sem, detour_sem,
    ):
        me = lax.axis_index("lat")
        lev = lax.axis_index("lev")
        polar = (me < quarter) | (me >= lat_count - quarter)
        plain = jnp.logical_not(polar)
        partner = lax.rem(me + shift, lat_count)

        spans = (pl.ds(levels - 1, 1), pl.ds(levels - 2, 1), pl.ds(0, levels - 2))

        def load(index):
            span = spans[index]
            return (
                pltpu.make_async_copy(fields.at[0, span], cells.at[0, span], in_sem.at[2 * index]),
                pltpu.make_async_copy(velocity.at[:, span], wind.at[:, span], in_sem.at[2 * index + 1]),
            )

        others = pl.ds(1, nf - 1)
        load_others = pltpu.make_async_copy(fields.at[others], cells.at[others], in_sem.at[6])
        own_copy = pltpu.make_async_copy(row_owner, owners, in_sem.at[7])
        thick_copy = pltpu.make_async_copy(thickness, thick, in_sem.at[8])
        ground_copy = pltpu.make_async_copy(surface, ground, in_sem.at[9])

        barrier = pltpu.get_barrier_semaphore()
        first = me == 0
        last = me == lat_count - 1

        @pl.when(jnp.logical_not(last))
        def _():
            pl.semaphore_signal(barrier, inc=1, device_id={"lat": me + 1}, device_id_type=MESH)

        @pl.when(jnp.logical_not(first))
        def _():
            pl.semaphore_signal(barrier, inc=1, device_id={"lat": me - 1}, device_id_type=MESH)


        for by in range(1, lev_count):
            pl.semaphore_signal(
                barrier, inc=1, device_id={"lev": lax.rem(lev + by, lev_count)}, device_id_type=MESH
            )

        for by in (shift, quarter, lat_count - quarter):
            pl.semaphore_signal(
                barrier, inc=1, device_id={"lat": lax.rem(me + by, lat_count)}, device_id_type=MESH
            )

        own_copy.start()
        for index in range(3):
            for copy in load(index):
                copy.start()
        load_others.start()
        thick_copy.start()
        ground_copy.start()

        middle = 2 * quarter
        routes = (
            (0, quarter - 1, quarter + 4, levels // 2),
            (1, lat_count - quarter, middle + 2, levels // 2),
            (0, middle - 1, middle + 4, levels // 2),
            (1, middle, quarter + 2, levels // 2),
        )
        greetings = {}
        for side, sender, via, _ in routes:
            target = sender + (1, -1)[side]
            for one, other in ((sender, via), (via, target)):
                greetings.setdefault(one, []).append(other)
                greetings.setdefault(other, []).append(one)
        for here, friends in greetings.items():
            @pl.when(me == here)
            def _():
                for there in friends:
                    pl.semaphore_signal(
                        barrier, inc=1, device_id={"lat": there}, device_id_type=MESH
                    )

        row_ids = (me * rows + lax.broadcasted_iota(jnp.int32, (rows, LANES), 0)).astype(jnp.float32)
        lat_mid = -0.5 * math.pi + (row_ids + 0.5) * spacing
        metric = 1.0 / jnp.maximum(jnp.cos(lat_mid), 0.25)
        to_north = diffuse_lat * metric * jnp.cos(lat_mid + 0.5 * spacing)
        to_south = diffuse_lat * metric * jnp.cos(lat_mid - 0.5 * spacing)
        to_side = diffuse_lon * metric * metric
        tables[0] = 0.5 * courant_lon * metric
        tables[1] = to_side
        tables[2] = to_north
        tables[3] = to_south
        tables[4] = 1.0 - 2.0 * to_side - to_north - to_south

        lane = lax.broadcasted_iota(jnp.int32, (SUBS, LANES), 1)
        for place in range(SLACK):
            at = (segment + 2 * PAD + place) * SUBS
            front[at : at + SUBS, :] = jnp.zeros((SUBS, LANES), jnp.float32)

        own_copy.wait()
        sent, kept = [], []
        for row in range(rows):
            away = (owners[row] != me).astype(jnp.int32)
            sent.append(away + (sent[-1] if row else 0))
            kept.append(row + 1 - sent[-1])

        def fill_slots(counts, base):
            for slot in range(half):
                place = jnp.int32(slot)
                for row in range(slot, slot + half):
                    place = place + (counts[row] <= slot).astype(jnp.int32)
                slots[base + slot] = place

        fill_slots(sent, 0)

        every = pl.ds(0, levels)
        edge = (pl.ds(rows - 1, 1), pl.ds(0, 1))

        def halo_copy(side, span):
            return pltpu.make_async_remote_copy(
                src_ref=fields.at[:, span, edge[side], :], dst_ref=halo.at[side, :, span],
                send_sem=halo_sem.at[0], recv_sem=halo_sem.at[1],
                device_id={"lat": lax.rem(me + (1, lat_count - 1)[side], lat_count)}, device_id_type=MESH,
            )

        def pass_in(side, sender, via, count):
            return pltpu.make_async_remote_copy(
                src_ref=fields.at[:, pl.ds(0, count), edge[side], :], dst_ref=passing.at[:, pl.ds(0, count)],
                send_sem=halo_sem.at[0], recv_sem=pass_sem.at[0],
                device_id={"lat": via}, device_id_type=MESH,
            )

        def pass_out(side, sender, via, count):
            return pltpu.make_async_remote_copy(
                src_ref=passing.at[:, pl.ds(0, count)], dst_ref=halo.at[side, :, pl.ds(0, count)],
                send_sem=pass_sem.at[1], recv_sem=halo_sem.at[1],
                device_id={"lat": sender + (1, -1)[side]}, device_id_type=MESH,
            )

        own_south = pltpu.make_async_copy(fields.at[:, :, 0:1, :], halo.at[0], halo_sem.at[1])
        own_north = pltpu.make_async_copy(fields.at[:, :, rows - 1 : rows, :], halo.at[1], halo_sem.at[1])

        factor_copy = pltpu.make_async_remote_copy(
            src_ref=factor_out, dst_ref=factor, send_sem=factor_sem.at[0], recv_sem=factor_sem.at[1],
            device_id={"lat": partner}, device_id_type=MESH,
        )

        def row_copy(source, target, part, device=partner):
            return pltpu.make_async_remote_copy(
                src_ref=source, dst_ref=target, send_sem=send_sem.at[0], recv_sem=recv_sem.at[part],
                device_id={"lat": device}, device_id_type=MESH,
            )

        def early_copy(*place):
            return row_copy(packed.at[place], landed.at[place], place[0])

        def field_copy(q):
            return row_copy(packed.at[q], landed.at[q] if q < last_q else polar_rows.at[q], q)

        onward = lax.rem(me + quarter, lat_count)
        column = lax.rem(me, quarter) // 2
        turn = (last_q - 1, levels - 1, pl.ds(half - SUBS, SUBS))

        def detour_in(width):
            return pltpu.make_async_remote_copy(
                src_ref=packed.at[(*turn, pl.ds(0, width))], dst_ref=detour.at[:, pl.ds(0, width)],
                send_sem=send_sem.at[0], recv_sem=detour_sem.at[0],
                device_id={"lat": onward}, device_id_type=MESH,
            )

        def detour_out(width):
            return pltpu.make_async_remote_copy(
                src_ref=detour.at[:, pl.ds(0, width)], dst_ref=landed.at[(*turn, pl.ds(0, width))],
                send_sem=detour_sem.at[1], recv_sem=recv_sem.at[last_q - 1],
                device_id={"lat": onward}, device_id_type=MESH,
            )

        odd = lax.rem(column, 2) == 1
        detours = ((lons // 4, jnp.logical_not(odd)), (5 * lons // 8, odd))
        above = me >= lat_count - quarter
        under = me < quarter

        def col_copy(by):
            return pltpu.make_async_remote_copy(
                src_ref=below, dst_ref=columns.at[by - 1], send_sem=col_sem.at[0], recv_sem=col_sem.at[1],
                device_id={"lev": lax.rem(lev + lev_count - by, lev_count)}, device_id_type=MESH,
            )

        def col_copies(n):
            return pltpu.make_async_remote_copy(
                src_ref=columns.at[pl.ds(0, n)], dst_ref=columns.at[pl.ds(0, n)],
                send_sem=col_sem.at[0], recv_sem=col_sem.at[1],
                device_id={"lev": lax.rem(lev + 1, lev_count)}, device_id_type=MESH,
            )

        def halo_copies(ref):
            return pltpu.make_async_remote_copy(
                src_ref=ref, dst_ref=ref, send_sem=halo_sem.at[0], recv_sem=halo_sem.at[1],
                device_id={"lat": partner}, device_id_type=MESH,
            )

        sub = lax.broadcasted_iota(jnp.int32, (SUBS, CHUNK), 0)

        def advect_chunk(q, k, part, edges):
            cols = pl.ds(pl.multiple_of(part * CHUNK, LANES), CHUNK)
            left = pl.ds(pl.multiple_of(lax.rem(part * per + blocks - 1, blocks) * LANES, LANES), LANES)
            right = pl.ds(pl.multiple_of(lax.rem((part + 1) * per, blocks) * LANES, LANES), LANES)

            def spread(table, group):
                one = tables[table, group * SUBS : (group + 1) * SUBS, :]
                return jnp.concatenate([one] * per, axis=1)

            state = [cells[q, k, g * SUBS : (g + 1) * SUBS, cols] for g in range(groups)]
            up = [pltpu.roll(one, SUBS - 1, 0) for one in state]
            if edges:
                up.append(jnp.broadcast_to(halo[1, q, k, :, cols], (SUBS, CHUNK)))
                down = [jnp.broadcast_to(halo[0, q, k, :, cols], (SUBS, CHUNK))]
            else:
                up.append(state[groups - 1])
                down = [state[0]]
            down += [pltpu.roll(one, 1, 0) for one in state]
            for g in range(groups):
                span = pl.ds(g * SUBS, SUBS)
                wide = CHUNK + LANES
                east = pltpu.roll(jnp.concatenate([state[g], cells[q, k, span, right]], axis=1), wide - 1, 1)
                west = pltpu.roll(jnp.concatenate([cells[q, k, span, left], state[g]], axis=1), 1, 1)
                east, west = east[:, :CHUNK], west[:, LANES:]
                north = jnp.where(sub == SUBS - 1, up[g + 1], up[g])
                south = jnp.where(sub == 0, down[g], down[g + 1])
                along = spread(0, g) * wind[0, k, span, cols]
                across = (0.5 * courant_lat) * wind[1, k, span, cols]
                side = spread(1, g)
                result = (
                    spread(4, g) * state[g]
                    + ((side - along) * east + (side + along) * west)
                    + ((spread(2, g) - across) * north + (spread(3, g) + across) * south)
                )
                new_fields[q, k, span, cols] = result

        def advect_level(q, k, edges):
            def one(part, carry):
                advect_chunk(q, k, part, edges)
                return carry

            lax.fori_loop(0, chunks, one, 0)

        def pack(q, k, chosen, start=0, cols=slice(None)):
            for place, slot in enumerate(chosen):
                packed[q, k, start + place : start + place + 1, cols] = new_fields[
                    q, k, pl.ds(slots[slot], 1), cols
                ]

        def keep(q, k):
            for slot in range(half):
                polar_rows[q, k, slot : slot + 1, :] = new_fields[q, k, pl.ds(slots[half + slot], 1), :]

        def first_level(k):
            advect_level(0, k, False)

            @pl.when(polar)
            def _():
                pack(0, k, order[:SUBS])

        def send_first(k):
            @pl.when(polar)
            def _():
                early_copy(0, k, pl.ds(0, SUBS)).start()

        for copy in load(0):
            copy.wait()
        first_level(levels - 1)

        heard = 5 + lev_count - 1 - (first | last).astype(jnp.int32)
        for here, friends in greetings.items():
            heard = heard + (me == here).astype(jnp.int32) * len(friends)
        pl.semaphore_wait(barrier, heard)
        send_first(levels - 1)

        for side, end in ((0, last), (1, first)):
            whole = jnp.logical_not(end)
            for route in routes:
                if route[0] == side:
                    whole = whole & (me != route[1])

            @pl.when(whole)
            def _():
                halo_copy(side, every).start()

        for route in routes:
            @pl.when(me == route[1])
            def _():
                pass_in(*route).start()
                halo_copy(route[0], pl.ds(route[3], levels - route[3])).start()

        @pl.when(first)
        def _():
            own_south.start()

        @pl.when(last)
        def _():
            own_north.start()

        def other_levels(index, carry):
            k = levels - 2 - index
            for stage in range(1, 3):
                @pl.when(index == stage - 1)
                def _():
                    for copy in load(stage):
                        copy.wait()

            first_level(k)
            send_first(k)
            return carry

        lax.fori_loop(0, levels - 1, other_levels, 0)

        @pl.when(polar)
        def _():
            here = lax.rem(lane, rows)
            away = jnp.zeros((SUBS, LANES), jnp.int32)
            slot_of = lax.rem(lane, half)
            for place, slot in enumerate(order):
                away = jnp.where(slot_of == place, slots[slot], away)
            factor[...] = strength_of((me * rows + here).astype(jnp.float32), all_rows)
            factor_out[...] = strength_of((me * rows + away).astype(jnp.float32), all_rows)

        @pl.when(polar)
        def _():
            factor_copy.start()

        for route in routes:
            @pl.when(me == route[2])
            def _():
                pass_in(*route).wait_recv()
                pass_out(*route).start()

        halo_copies(halo).wait_recv()

        def mend_edges(k, part):
            cols = pl.ds(pl.multiple_of(part * CHUNK, LANES), CHUNK)
            for side, group, line, sign in ((0, 0, 0, 1.0), (1, groups - 1, SUBS - 1, -1.0)):
                span = pl.ds(group * SUBS, SUBS)
                table = tables[3 - side, span, :]
                weight = (
                    jnp.concatenate([table] * per, axis=1)
                    + (sign * 0.5 * courant_lat) * wind[1, k, span, cols]
                )
                beyond = jnp.broadcast_to(halo[side, 0, k, :, cols], (SUBS, CHUNK))
                change = weight * (beyond - cells[0, k, span, cols])
                new_fields[0, k, span, cols] = new_fields[0, k, span, cols] + jnp.where(
                    sub == line, change, 0.0
                )

        def mend_level(index, carry):
            k = levels - 1 - index

            def one(part, carry):
                mend_edges(k, part)
                return carry

            lax.fori_loop(0, chunks, one, 0)

            @pl.when(polar)
            def _():
                pack(0, k, order[SUBS:], SUBS)

            return carry

        lax.fori_loop(0, levels, mend_level, 0)

        @pl.when(polar)
        def _():
            early_copy(0, slice(None), pl.ds(SUBS, half - SUBS)).start()

        thick_copy.wait()

        def add_levels(index, carry):
            cols = pl.ds(pl.multiple_of(index * CHUNK, LANES), CHUNK)
            for group in range(groups):
                span = pl.ds(group * SUBS, SUBS)
                so_far = jnp.zeros((SUBS, CHUNK), jnp.float32)
                for k in reversed(range(levels)):
                    weight = (base_temp + new_fields[0, k, span, cols]) * thick[k]
                    geo[k, span, cols] = so_far + 0.5 * weight
                    so_far = so_far + weight
                below[span, cols] = so_far
            return carry

        lax.fori_loop(0, chunks, add_levels, 0)

        for by in range(1, lev_count):
            @pl.when(lev >= by)
            def _():
                col_copy(by).start()

        fill_slots(kept, half)

        load_others.wait()

        def next_field(index, carry):
            q = 1 + index // levels
            k = levels - 1 - lax.rem(index, levels)
            advect_level(q, k, True)

            @pl.when(polar & (q < last_q))
            def _():
                pack(q, k, order)

            return carry

        lax.fori_loop(0, levels, next_field, 0)

        for width, chosen in detours:
            @pl.when(above & chosen)
            def _():
                detour_in(width).start()
                early_copy(*turn, pl.ds(width, lons - width)).start()

        @pl.when(polar & jnp.logical_not(above))
        def _():
            early_copy(*turn, slice(None)).start()

        @pl.when(polar)
        def _():
            early_copy(last_q - 1, levels - 1, pl.ds(0, half - SUBS)).start()
            early_copy(last_q - 1, pl.ds(0, levels - 1)).start()

        lax.fori_loop(levels, slabs - levels, next_field, 0)

        for width, chosen in detours:
            @pl.when(under & chosen)
            def _():
                detour_in(width).wait_recv()
                detour_out(width).start()

        def place_of(block):
            return lax.rem(block, per_segment) * LANES + PAD, block // per_segment

        def run(place):
            return pl.ds(pl.multiple_of(place * SUBS, SUBS), SUBS)

        def put_block(block, values):
            start, which = place_of(block)
            turned = values.T
            for v in range(LANES // SUBS):
                front[pl.ds((start + SUBS * v) * SUBS + which, SUBS, stride=SUBS), :] = turned[
                    SUBS * v : SUBS * (v + 1), :
                ]

        def get_block(block):
            start, which = place_of(block)
            return jnp.concatenate(
                [
                    front[pl.ds((start + SUBS * v) * SUBS + which, SUBS, stride=SUBS), :]
                    for v in range(LANES // SUBS)
                ],
                axis=0,
            ).T

        def cols_of(block):
            return pl.ds(pl.multiple_of(block * LANES, LANES), LANES)

        def one_pass(source, target, start, strength):
            def flux_of(west, slope, east):
                least = jnp.minimum(jnp.maximum(west, east), 0.0)
                most = jnp.maximum(jnp.minimum(west, east), 0.0)
                return strength * (slope - jnp.minimum(jnp.maximum(slope, least), most))

            def steps(index, state):
                cell, ahead, west, slope, inflow = state
                base = start + index * STEPS
                for j in range(STEPS):
                    beyond = source[run(base + j + 2), :]
                    east = beyond - ahead
                    outflow = flux_of(west, slope, east)
                    target[run(base + j), :] = cell + (outflow - inflow)
                    cell, ahead, west, slope, inflow = ahead, beyond, slope, east, outflow
                return cell, ahead, west, slope, inflow

            near = [source[run(start - 2 + j), :] for j in range(4)]
            slopes = [near[j + 1] - near[j] for j in range(3)]
            inflow = flux_of(slopes[0], slopes[1], slopes[2])
            lax.fori_loop(
                0, (length - SLACK) // STEPS, steps, (near[2], near[3], slopes[1], slopes[2], inflow)
            )

        def all_passes():
            for j in range(PAD):
                front[j * SUBS : (j + 1) * SUBS, :] = pltpu.roll(
                    front[(segment + j) * SUBS : (segment + j + 1) * SUBS, :], 1, 0
                )
                end = (PAD + segment + j) * SUBS
                front[end : end + SUBS, :] = pltpu.roll(
                    front[(PAD + j) * SUBS : (PAD + j + 1) * SUBS, :], SUBS - 1, 0
                )
            strength = factor[...]

            def pair(index, carry):
                one_pass(front, back, 2 + 4 * index, strength)
                one_pass(back, front, 4 + 4 * index, strength)
                return carry

            lax.fori_loop(0, PASSES // 2, pair, 0)

        @pl.when(plain)
        def _():
            factor_copy.wait_recv()

        def job(index, carry):
            q = lax.rem(index + last_q, nf)

            @pl.when(polar)
            def _():
                def fill(index, carry):
                    for block in (index * UNROLL + i for i in range(UNROLL)):
                        values = new_fields[q, :, :, cols_of(block)]
                        put_block(block, values.reshape(LANES, LANES))
                    return carry

                lax.fori_loop(0, blocks // UNROLL, fill, 0)

            @pl.when(plain & (index < last_q))
            def _():
                for q in range(last_q):
                    @pl.when(index == q)
                    def _():
                        field_copy(q).wait_recv()

                def fill(place, carry):
                    for block in (place * UNROLL + i for i in range(UNROLL)):
                        values = landed[index, :, :, cols_of(block)].reshape(levels * half, LANES)
                        put_block(block, jnp.concatenate([values, values], axis=0))
                    return carry

                lax.fori_loop(0, blocks // UNROLL, fill, 0)

            @pl.when(polar | (index < last_q))
            def _():
                all_passes()

            @pl.when(polar)
            def _():
                def spill(place, carry):
                    for block in (place * UNROLL + i for i in range(UNROLL)):
                        new_fields[q, :, :, cols_of(block)] = get_block(block).reshape(
                            levels, rows, LANES
                        )
                    return carry

                lax.fori_loop(0, blocks // UNROLL, spill, 0)

                @pl.when(index == 0)
                def _():
                    def send(k, carry):
                        pack(last_q, k, range(half))
                        return carry

                    lax.fori_loop(0, levels, send, 0)
                    field_copy(last_q).start()

                def hold(k, carry):
                    keep(q, k)
                    return carry

                lax.fori_loop(0, levels, hold, 0)

            @pl.when(plain & (index < last_q))
            def _():
                def spill(place, carry):
                    for block in (place * UNROLL + i for i in range(UNROLL)):
                        values = get_block(block)
                        for k in range(levels):
                            one = values[k * half : (k + 1) * half, :]
                            whole = jnp.concatenate([one[half - 2 : half - 1], one[: half - 2], one[half - 1 :]], axis=0)
                            polar_rows[index, k, :, cols_of(block)] = whole
                    return carry

                lax.fori_loop(0, blocks // UNROLL, spill, 0)

            return carry

        lax.fori_loop(0, nf, job, 0)

        ground_copy.wait()
        for n in range(1, lev_count):
            @pl.when(lev == lev_count - 1 - n)
            def _():
                col_copies(n).wait_recv()

        def finish(index, carry):
            span = pl.ds(pl.multiple_of(index * SUBS, SUBS), SUBS)
            outside = ground[span, :]
            for by in range(1, lev_count):
                outside = outside + jnp.where(lev + by < lev_count, columns[by - 1, span, :], 0.0)
            for k in range(levels):
                geo[k, span, :] = geo[k, span, :] + outside
            return carry

        lax.fori_loop(0, groups, finish, 0)

        for n in range(1, lev_count):
            @pl.when(lev == n)
            def _():
                col_copies(n).wait_send()

        @pl.when(first | last)
        def _():
            halo_copies(halo.at[0]).wait_send()

        @pl.when(jnp.logical_not(first | last))
        def _():
            halo_copies(halo).wait_send()

        for route in routes:
            @pl.when(me == route[2])
            def _():
                pass_out(*route).wait_send()

        for width, chosen in detours:
            @pl.when(under & chosen)
            def _():
                detour_out(width).wait_send()

        @pl.when(polar)
        def _():
            factor_copy.wait_send()
            row_copy(packed, polar_rows, last_q).wait_send()

        @pl.when(plain)
        def _():
            field_copy(last_q).wait_recv()

    return kernel


def write_out(new_fields, geo, polar_rows, new_fields_out, geo_out, polar_rows_out, sem):
    copies = [
        pltpu.make_async_copy(new_fields, new_fields_out, sem.at[0]),
        pltpu.make_async_copy(geo, geo_out, sem.at[1]),
        pltpu.make_async_copy(polar_rows, polar_rows_out, sem.at[2]),
    ]
    for copy in copies:
        copy.start()
    for copy in copies:
        copy.wait()


def solution(mesh):
    lat_count, lev_count = mesh.shape["lat"], mesh.shape["lev"]

    def local(fields, velocity, surface, thickness, row_owner):
        nf, levels, rows, lons = fields.shape
        half = rows // 2
        length = lons // SUBS + 2 * PAD + SLACK
        hbm_spec = pl.BlockSpec(memory_space=pltpu.HBM)
        vmem_spec = pl.BlockSpec(memory_space=pltpu.VMEM)
        dma = pltpu.SemaphoreType.DMA
        f32 = jnp.float32
        shapes = ((nf, levels, rows, lons), (levels, rows, lons), (nf, levels, half, lons))
        held_bytes = sum(4 * math.prod(shape) for shape in shapes)
        held = pl.pallas_call(
            make_kernel(lat_count, lev_count, nf, levels, rows, lons),
            out_shape=tuple(pltpu.VMEM(shape, f32) for shape in shapes),
            in_specs=[hbm_spec] * 5,
            out_specs=[vmem_spec] * 3,
            scratch_shapes=[
                pltpu.VMEM((nf, levels, rows, lons), f32),
                pltpu.VMEM((2, levels, rows, lons), f32),
                pltpu.VMEM((rows, lons), f32),
                pltpu.VMEM((2, nf, levels, 1, lons), f32),
                pltpu.VMEM((rows, lons), f32),
                pltpu.VMEM((lev_count - 1, rows, lons), f32),
                pltpu.VMEM((nf, levels, half, lons), f32),
                pltpu.VMEM((nf - 1, levels, half, lons), f32),
                pltpu.VMEM((length * SUBS, LANES), f32),
                pltpu.VMEM((length * SUBS, LANES), f32),
                pltpu.VMEM((5, rows, LANES), f32),
                pltpu.VMEM((SUBS, LANES), f32),
                pltpu.VMEM((SUBS, LANES), f32),
                pltpu.SMEM((rows,), jnp.int32),
                pltpu.SMEM((levels,), f32),
                pltpu.SMEM((rows,), jnp.int32),
                pltpu.VMEM((SUBS, 5 * lons // 8), f32),
                pltpu.VMEM((nf, levels // 2, 1, lons), f32),
                dma((2,)),
                dma((10,)),
                dma((2,)),
                dma((2,)),
                dma((1,)),
                dma((nf,)),
                dma((2,)),
                dma((2,)),
            ],
            compiler_params=pltpu.CompilerParams(
                collective_id=0, has_side_effects=True, vmem_limit_bytes=67043328 - held_bytes
            ),
            name="step",
        )(fields, velocity, surface, thickness, row_owner)
        return pl.pallas_call(
            write_out,
            out_shape=tuple(jax.ShapeDtypeStruct(shape, f32) for shape in shapes),
            in_specs=[pl.BlockSpec(memory_space=pl.ANY)] * 3,
            out_specs=[hbm_spec] * 3,
            scratch_shapes=[dma((3,))],
            compiler_params=pltpu.CompilerParams(vmem_limit_bytes=1024 * 1024),
            name="write",
        )(*held)

    in_specs = (
        P(None, "lev", "lat", None),
        P(None, "lev", "lat", None),
        P("lat", None),
        P("lev"),
        P("lat"),
    )
    out_specs = (P(None, "lev", "lat", None), P("lev", "lat", None), P(None, "lev", "lat", None))
    return jax.shard_map(local, mesh=mesh, in_specs=in_specs, out_specs=out_specs, check_vma=False)
```
